128 devices in a mesh: gx: 8 (over z, x_hi), gy: 4 (over y), gz: 4 (over x_lo, core).
Axes of the slice: x: 4 (x_hi: 2, x_lo: 2; x = x_hi * 2 + x_lo), y: 4, z: 4, core: 2. Of those that a mesh axis runs over, the one named last changes fastest.
Arguments:
- velocity: float32 [3, 128, 128, 512], P(None, 'gx', 'gy', 'gz'), may hold values from -5 to 5
- target_visc: bfloat16 [128, 128, 512], P('gx', 'gy', 'gz'), may hold values from 0.0099487305 to 0.29882812
- weight_in: bfloat16 [128, 10], replicated, may hold values from -2 to 2
- bias_in: float32 [128], replicated, may hold values from -3 to 3
- weight_mid: bfloat16 [128, 128], replicated, may hold values from -0.5 to 0.5
- bias_mid: float32 [128], replicated, may hold values from -3 to 3
- weight_out: bfloat16 [128], replicated, may hold values from -0.5 to 0.5
- patch_count: int32 [8, 4, 4], P('gx', 'gy', 'gz'), may hold values from 4 to 8, as said below
- patch_corner: int32 [8, 4, 4, 8, 3], P('gx', 'gy', 'gz'), may hold values from 0 to 112, as said below
- patch_dest: int32 [8, 4, 4, 8], P('gx', 'gy', 'gz'), may hold values from 0 to 3, as said below
Outputs:
- new_velocity: float32 [3, 128, 128, 512], P(None, 'gx', 'gy', 'gz')
- grad_weight_in: float32 [128, 10], replicated
- grad_bias_in: float32 [128], replicated
- grad_weight_mid: float32 [128, 128], replicated
- grad_bias_mid: float32 [128], replicated
- grad_weight_out: float32 [128], replicated
The draws below stay inside these ranges and needn't reach their ends.
Inputs may be any that keep to these rules, and one draw needn't show every extreme that they name: `patch_count`: bricks at either wall have all 8 slots live; the others have at least half of them live. `patch_corner`: entries along the last dimension are the corner's offsets along the first, second and third grid dimension inside the brick, so that every patch of 16 cells a side lies inside its brick. `patch_dest`: each brick sends exactly 2 of its 8 slots to each trainer index k, live or not; trainer k of a gx index is the device with gy index k and gz index k.
All inputs are finite; a program needn't handle non-finite values.
Results may differ from the reference program's by a relative error of at most 0.0003.
Values may be sent and summed in bfloat16 or wider, within the bound.
No kernel may reach another device: no remote copies, remote signals or barrier semaphores. Data moves between devices by JAX's collectives and lax.ppermute only.
A program may use at most 64 MiB of HBM per device.

```python
import math
import jax
import jax.numpy as jnp
from jax import lax

CX = 16
CY = 32
CZ = 128
HID = 128
FEAT = 10
PATCH = 16
CAP = 2
NX = 128
NY = 128
NZ = 512
N_GX = 8
N_GY = 4
N_GZ = 4


def draw_patch_count(key, part):
    slot_total = CAP * N_GZ
    interior = jax.random.randint(key, (N_GX, N_GY, N_GZ), slot_total // 2, slot_total + 1)
    rows_y = jnp.arange(N_GY, dtype=jnp.int32)[None, :, None]
    at_wall = (rows_y == 0) | (rows_y == N_GY - 1)
    return jnp.where(at_wall, slot_total, interior).astype(jnp.int32)


def draw_patch_corner(key, part):
    slot_total = CAP * N_GZ
    subkeys = jax.random.split(jax.random.fold_in(key, 11), 4)
    draw_shape = (N_GX, N_GY, N_GZ, slot_total)
    corner_x = jax.random.randint(subkeys[0], draw_shape, 0, CX - PATCH + 1)
    corner_z = jax.random.randint(subkeys[1], draw_shape, 0, CZ - PATCH + 1)
    first_draw = jax.random.randint(subkeys[2], draw_shape, 0, CY - PATCH + 1)
    second_draw = jax.random.randint(subkeys[3], draw_shape, 0, CY - PATCH + 1)
    rows_y = jnp.arange(N_GY, dtype=jnp.int32)[None, :, None, None]
    lower = jnp.minimum(first_draw, second_draw)
    upper = jnp.maximum(first_draw, second_draw)
    corner_y = jnp.where(rows_y == 0, lower, jnp.where(rows_y == N_GY - 1, upper, first_draw))
    return jnp.stack([corner_x, corner_y, corner_z], -1).astype(jnp.int32)


def draw_patch_dest(key, part):
    slot_total = CAP * N_GZ
    scores = jax.random.randint(jax.random.fold_in(key, 23), (N_GX, N_GY, N_GZ, slot_total), 0, 1 << 20)
    scores = scores * slot_total + jnp.arange(slot_total, dtype=jnp.int32)
    slot_order = jnp.argsort(scores, axis=-1, stable=True)
    return (slot_order // CAP).astype(jnp.int32)


def block_scale(stream_key, shape, shards, low, top_value):
    level = 1.0
    for axis_at, parts in shards:
        steps = jax.random.uniform(jax.random.fold_in(jax.random.fold_in(stream_key, 6), axis_at), (parts,), jnp.float32, low / len(shards), top_value / len(shards))
        level = level * jnp.repeat(jnp.exp(steps), shape[axis_at] // parts).reshape((-1,) + (1,) * (len(shape) - 1 - axis_at))
    return level


def noise(key, extent, width, bound, cuts=(), kind=jnp.bfloat16):
    drawn = jax.random.normal(key, extent, jnp.float32) * width
    if len(cuts) > 0:
        drawn = block_scale(key, extent, cuts, -0.22, 0.18) * drawn
    return jnp.clip(drawn, min=-bound, max=bound).astype(kind)


def setup_inputs(seed: int = 0) -> dict:
    seeds = jax.random.split(jax.random.key(seed), 11)
    return {
        "velocity": noise(seeds[0], (3, NX, NY, NZ), 1.0, 5.0, ((1, 8), (2, 4), (3, 4)), jnp.float32),
        "target_visc": jnp.clip(jnp.exp(math.log(0.29882812) - 3.4024236 * jax.random.uniform(seeds[1], (NX, NY, NZ), jnp.float32) ** block_scale(seeds[1], (NX, NY, NZ), ((0, 8), (1, 4), (2, 4)), -0.2, 0.2)), 0.0099487305, 0.29882812).astype(jnp.bfloat16),
        "weight_in": noise(seeds[2], (HID, FEAT), FEAT ** -0.5, 2.0),
        "bias_in": noise(seeds[3], (HID,), 0.5, 3.0, (), jnp.float32),
        "weight_mid": noise(seeds[4], (HID, HID), HID ** -0.5, 0.5),
        "bias_mid": noise(seeds[5], (HID,), 0.5, 3.0, (), jnp.float32),
        "weight_out": noise(seeds[6], (HID,), HID ** -0.5, 0.5),
        "patch_count": draw_patch_count(jax.random.fold_in(seeds[10], 71), 0),
        "patch_corner": draw_patch_corner(jax.random.fold_in(seeds[10], 71), 0),
        "patch_dest": draw_patch_dest(jax.random.fold_in(seeds[10], 71), 0),
    }


time_step = 0.2
base_viscosity = 0.02
eddy_scale = 0.1
grad_gain = 20.0
norm_epsilon = 1e-06

def mlp_forward(features, weight_in, bias_in, weight_mid, bias_mid, weight_out):
    pre_one = jnp.dot(weight_in, features, preferred_element_type=jnp.float32) + bias_in[:, None]
    act_one = jnp.tanh(pre_one)
    hidden_one = act_one.astype(jnp.bfloat16)
    pre_two = jnp.dot(weight_mid, hidden_one, preferred_element_type=jnp.float32) + bias_mid[:, None]
    act_two = jnp.tanh(pre_two)
    hidden_two = act_two.astype(jnp.bfloat16)
    logit_out = jnp.dot(weight_out, hidden_two, preferred_element_type=jnp.float32)
    return (act_one, hidden_one, act_two, hidden_two, logit_out)

def eddy_field(flat_features, params, block_size):
    total_cells = flat_features.shape[1]

    def one_block(block_index):
        start = (block_index * block_size).astype(jnp.int32)
        piece = lax.dynamic_slice_in_dim(flat_features, start, block_size, 1)
        logit_out = mlp_forward(piece, *params)[4]
        return eddy_scale * jax.nn.softplus(logit_out)
    blocks = lax.map(one_block, jnp.arange(total_cells // block_size, dtype=jnp.int32))
    return blocks.reshape(total_cells)

def tendency(widened, params, wall_field, block_size):
    center = widened[:, 1:-1, 1:-1, 1:-1]
    diff_x = (widened[:, 2:, 1:-1, 1:-1] - widened[:, :-2, 1:-1, 1:-1]) * 0.5
    diff_y = (widened[:, 1:-1, 2:, 1:-1] - widened[:, 1:-1, :-2, 1:-1]) * 0.5
    diff_z = (widened[:, 1:-1, 1:-1, 2:] - widened[:, 1:-1, 1:-1, :-2]) * 0.5
    laplace = widened[:, 2:, 1:-1, 1:-1] + widened[:, :-2, 1:-1, 1:-1]
    laplace = laplace + widened[:, 1:-1, 2:, 1:-1] + widened[:, 1:-1, :-2, 1:-1]
    laplace = laplace + widened[:, 1:-1, 1:-1, 2:] + widened[:, 1:-1, 1:-1, :-2] - 6.0 * center
    features = jnp.concatenate([diff_x, diff_y, diff_z, wall_field], 0).astype(jnp.bfloat16)
    flat_features = features.reshape(features.shape[0], -1)
    eddy_visc = eddy_field(flat_features, params, block_size).reshape(center.shape[1:])
    advect = center[0][None] * diff_x + center[1][None] * diff_y + center[2][None] * diff_z
    section_rate = -advect + (base_viscosity + eddy_visc)[None] * laplace
    return (section_rate, features)

def mlp_grads(features, target, weight, params):
    weight_in, bias_in, weight_mid, bias_mid, weight_out = params
    act_one, hidden_one, act_two, hidden_two, logit_out = mlp_forward(features, *params)
    eddy_visc = eddy_scale * jax.nn.softplus(logit_out)
    delta_out = (weight * (eddy_visc - target.astype(jnp.float32)) * eddy_scale * jax.nn.sigmoid(logit_out)).astype(jnp.bfloat16)
    grad_out = jnp.dot(hidden_two, delta_out, preferred_element_type=jnp.float32)
    delta_two = (weight_out.astype(jnp.float32)[:, None] * delta_out.astype(jnp.float32)[None, :] * (1.0 - act_two * act_two)).astype(jnp.bfloat16)
    grad_mid = jnp.dot(delta_two, hidden_one.T, preferred_element_type=jnp.float32)
    bias_two = lax.optimization_barrier(jnp.sum(delta_two.astype(jnp.float32), axis=1))
    back_one = jnp.dot(weight_mid.T, delta_two, preferred_element_type=jnp.float32)
    delta_one = (back_one * (1.0 - act_one * act_one)).astype(jnp.bfloat16)
    grad_in = jnp.dot(delta_one, features.T, preferred_element_type=jnp.float32)
    bias_one = lax.optimization_barrier(jnp.sum(delta_one.astype(jnp.float32), axis=1))
    return (grad_in, bias_one, grad_mid, bias_two, grad_out)

def patch_grads(payload, live_flags, params):
    channels, patch_total, patch_cells = payload.shape
    feat_count = channels - 1

    def add_pair(block_index, running):
        start = (block_index * 2).astype(jnp.int32)
        pair_block = lax.dynamic_slice_in_dim(payload, start, 2, 1)
        alive_pair = lax.dynamic_slice_in_dim(live_flags, start, 2, 0)
        features = pair_block[:feat_count].reshape(feat_count, 2 * patch_cells)
        target = pair_block[feat_count].reshape(2 * patch_cells)
        weight = jnp.repeat(alive_pair, patch_cells)
        grad_terms = mlp_grads(features, target, weight, params)
        return tuple((earlier + addend for earlier, addend in zip(running, grad_terms)))
    initial = tuple((jnp.zeros(param.shape, jnp.float32) for param in params))
    return lax.fori_loop(0, patch_total // 2, add_pair, initial)

def slot_rank(targets):
    slot_order = jnp.arange(targets.shape[0], dtype=jnp.int32)
    same_target = (targets[:, None] == targets[None, :]) & (slot_order[None, :] < slot_order[:, None])
    return lax.optimization_barrier(jnp.sum(same_target.astype(jnp.int32), axis=1)).astype(jnp.int32)

def sort_patches(local_patches, live_slots, position, row_count):
    picker = (jnp.arange(row_count, dtype=jnp.int32)[:, None] == position[None, :]).astype(jnp.float32)
    ordered = jnp.einsum('rs,csp->crp', picker, local_patches.astype(jnp.float32)).astype(jnp.bfloat16)
    ordered_live = jnp.dot(picker, live_slots, precision=lax.Precision.HIGHEST)
    return (ordered, ordered_live)

def widen(field):
    padded = jnp.pad(field, ((0, 0), (1, 1), (0, 0), (1, 1)), mode='wrap')
    return jnp.pad(padded, ((0, 0), (0, 0), (1, 1), (0, 0)))

def reference(velocity, target_visc, weight_in, bias_in, weight_mid, bias_mid, weight_out, patch_count, patch_corner, patch_dest):
    params = (weight_in, bias_in, weight_mid, bias_mid, weight_out)
    block_size = min(8192, CX * CY * CZ)
    y_rows = jnp.arange(NY, dtype=jnp.float32)
    wall_line = 1.0 - jnp.abs(2.0 * (y_rows + 0.5) / NY - 1.0)
    wall_field = jnp.broadcast_to(wall_line[None, None, :, None], (1, NX, NY, NZ))
    rate_first, features = tendency(widen(velocity), params, wall_field, block_size)
    first_section = velocity + time_step * rate_first
    rate_second, unused = tendency(widen(first_section), params, wall_field, block_size)
    new_velocity = 0.5 * velocity + 0.5 * (first_section + time_step * rate_second)
    combined = jnp.concatenate([features, target_visc[None]], 0)
    slot_total = CAP * N_GZ
    trainers = N_GX * N_GZ
    initial = tuple((jnp.zeros((trainers,) + param.shape, jnp.float32) for param in params))

    def per_brick(running, brick_index):
        brick_x = brick_index // (N_GY * N_GZ)
        brick_y = brick_index // N_GZ % N_GY
        brick_z = brick_index % N_GZ
        live_total = patch_count[brick_x, brick_y, brick_z]
        corners = patch_corner[brick_x, brick_y, brick_z]
        targets = patch_dest[brick_x, brick_y, brick_z]
        live_slots = (jnp.arange(slot_total, dtype=jnp.int32) < live_total).astype(jnp.float32)
        pieces = []
        for slot_index in range(slot_total):
            anchor = (jnp.int32(0), (brick_x * CX + corners[slot_index, 0]).astype(jnp.int32), (brick_y * CY + corners[slot_index, 1]).astype(jnp.int32), (brick_z * CZ + corners[slot_index, 2]).astype(jnp.int32))
            cube = lax.dynamic_slice(combined, anchor, (FEAT + 1, PATCH, PATCH, PATCH))
            pieces.append(cube.reshape(FEAT + 1, PATCH ** 3))
        local_patches = jnp.stack(pieces, 1)
        position = (targets * CAP + slot_rank(targets)).astype(jnp.int32)
        ordered, ordered_live = sort_patches(local_patches, live_slots, position, slot_total)
        for group_index in range(N_GZ):
            grads = patch_grads(ordered[:, group_index * CAP:(group_index + 1) * CAP], ordered_live[group_index * CAP:(group_index + 1) * CAP], params)
            row_index = (brick_x * N_GZ + group_index).astype(jnp.int32)
            running = tuple((earlier.at[row_index].add(addend) for earlier, addend in zip(running, grads)))
        return (running, None)
    totals, unused = lax.scan(per_brick, initial, jnp.arange(N_GX * N_GY * N_GZ, dtype=jnp.int32))
    square = totals[0].sum(axis=(1, 2)) * 0.0
    for running in totals:
        square = square + lax.optimization_barrier(jnp.sum(running * running, axis=tuple(range(1, running.ndim))))
    factor_norm = grad_gain / jnp.sqrt(square + norm_epsilon)
    outputs = tuple((lax.optimization_barrier(jnp.sum(running * factor_norm.reshape((-1,) + (1,) * (running.ndim - 1)), axis=0)) for running in totals))
    return (new_velocity, outputs[0], outputs[1], outputs[2], outputs[3], outputs[4])
```

```python
import jax
import jax.numpy as jnp
from jax import lax
from jax.experimental import pallas as pl
from jax.experimental.pallas import tpu as pltpu
from jax.sharding import PartitionSpec as P

SX, SY, SZ = 16, 32, 128
HID = 128
FEAT = 10
PATCH = 16
CAP = 2
TRAINERS = 4
SLOTS = CAP * TRAINERS
ROWS = 160
QROWS = ROWS // 4
WIDE = 2 * SZ

time_step = 0.2
base_viscosity = 0.02
eddy_scale = 0.1
grad_gain = 20.0
norm_epsilon = 1e-06

f32 = jnp.float32
bf16 = jnp.bfloat16


def lanes_of(shape):
    return lax.broadcasted_iota(jnp.int32, shape, len(shape) - 1)


def sublanes_of(shape):
    return lax.broadcasted_iota(jnp.int32, shape, len(shape) - 2)


def softplus(x):
    return jnp.maximum(x, 0.0) + jnp.log1p(jnp.exp(-jnp.abs(x)))


def sigmoid(x):
    e = jnp.exp(-jnp.abs(x))
    return jnp.where(x >= 0, 1.0, e) / (1.0 + e)


def dot(a, b):
    return lax.dot_general(a, b, (((1,), (0,)), ((), ())), preferred_element_type=f32)


def dot_nt(a, b):
    return lax.dot_general(a, b, (((1,), (1,)), ((), ())), preferred_element_type=f32)


def wall_plane(gy):
    rows = (gy * SY + sublanes_of((SY, SZ))).astype(f32)
    return 1.0 - jnp.abs(2.0 * (rows + 0.5) / (SY * 4) - 1.0)


def put_faces(x, planes, xlo, xhi, ylo, yhi, zlo, zhi):
    lane = lanes_of((SY, SZ))
    low, high = zlo[...], zhi[...]
    for c in range(3):
        plane = planes[c]
        ylo[c, pl.ds(x, 1), :] = plane[0:1]
        yhi[c, pl.ds(x, 1), :] = plane[SY - 1 : SY]
        here = lane == c * SX + x
        low = jnp.where(here, jnp.broadcast_to(plane[:, 0:1], (SY, SZ)), low)
        high = jnp.where(here, jnp.broadcast_to(plane[:, SZ - 1 : SZ], (SY, SZ)), high)
    zlo[...] = low
    zhi[...] = high


def faces_kernel(v, xlo, xhi, ylo, yhi, zlo, zhi):
    zlo[...] = jnp.zeros((SY, SZ), f32)
    zhi[...] = jnp.zeros((SY, SZ), f32)
    xlo[...] = v[:, 0]
    xhi[...] = v[:, SX - 1]

    def step(x, carry):
        put_faces(x, [v[c, x] for c in range(3)], xlo, xhi, ylo, yhi, zlo, zhi)
        return carry

    lax.fori_loop(0, SX, step, 0)


FACE_SHAPES = ((3, SY, SZ),) * 2 + ((3, SX, SZ),) * 2 + ((SY, SZ),) * 2


def face_structs():
    return [jax.ShapeDtypeStruct(s, f32) for s in FACE_SHAPES]


def whole(n):
    return [pl.BlockSpec(memory_space=pltpu.VMEM) for _ in range(n)]


def smem(n):
    return [pl.BlockSpec(memory_space=pltpu.SMEM) for _ in range(n)]


def pack_faces(v):
    return pl.pallas_call(
        faces_kernel, out_shape=face_structs(), in_specs=whole(1), out_specs=whole(6), name="faces"
    )(v)


def exchange(faces):
    xlo, xhi, ylo, yhi, zlo, zhi = faces

    def shift(low, high, axis, closed):
        count = lax.axis_size(axis)
        ends = count if closed else count - 1
        from_low = lax.ppermute(high, axis, [(i, (i + 1) % count) for i in range(ends)])
        from_high = lax.ppermute(low, axis, [((i + 1) % count, i) for i in range(ends)])
        return from_low, from_high

    return (
        shift(xlo, xhi, "gx", True) + shift(ylo, yhi, "gy", False) + shift(zlo, zhi, "gz", True)
    )


def fill_padded(v, halos, pad):
    hx0, hx1, hy0, hy1 = halos[:4]
    for c in range(3):
        pad[c, 0, 8 : 8 + SY] = hx0[c]
        pad[c, SX + 1, 8 : 8 + SY] = hx1[c]

    def step(x, carry):
        for c in range(3):
            pad[c, x + 1, 8 : 8 + SY] = v[c, x]
            pad[c, x + 1, 7:8] = hy0[c, pl.ds(x, 1), :]
            pad[c, x + 1, 8 + SY : 9 + SY] = hy1[c, pl.ds(x, 1), :]
        return carry

    lax.fori_loop(0, SX, step, 0)


def stencil(x, pad, hz0, hz1):
    lane = lanes_of((SY, SZ))
    low, high = hz0[...], hz1[...]
    centers, dxs, dys, dzs, laps = [], [], [], [], []
    for c in range(3):
        at = c * SX + x
        ctr = pad[c, x + 1, 8 : 8 + SY]
        xm, xp = pad[c, x, 8 : 8 + SY], pad[c, x + 2, 8 : 8 + SY]
        ym, yp = pad[c, x + 1, 7 : 7 + SY], pad[c, x + 1, 9 : 9 + SY]
        zm = jnp.where(lane == 0, pltpu.roll(low, (SZ - at) % SZ, 1), pltpu.roll(ctr, 1, 1))
        zp = jnp.where(
            lane == SZ - 1, pltpu.roll(high, SZ - 1 - at, 1), pltpu.roll(ctr, SZ - 1, 1)
        )
        centers.append(ctr)
        dxs.append((xp - xm) * 0.5)
        dys.append((yp - ym) * 0.5)
        dzs.append((zp - zm) * 0.5)
        laps.append(xp + xm + yp + ym + zp + zm - 6.0 * ctr)
    return centers, dxs, dys, dzs, laps


def columns(channels, group):
    parts = [ch[group * 8 : group * 8 + 8] for ch in channels]
    parts.append(jnp.ones((16, SZ), f32))
    return jnp.concatenate(parts, 0).astype(bf16)


def section_kernel(second, *refs):
    gy = refs[0]
    v, *halos = refs[1:8]
    at = 8
    if second:
        velocity = refs[at]
        at += 1
    first_w, mid_w, out_w = refs[at : at + 3]
    at += 3
    new = refs[at]
    at += 1
    if not second:
        faces = refs[at : at + 6]
        at += 6
    pad, h_one_s, h_two_s = refs[at : at + 3]
    fill_padded(v, halos, pad)
    wall = wall_plane(gy[0])
    h_one_s[HID : HID + 16] = jnp.ones((16, 16 * WIDE), bf16)
    if not second:
        faces[4][...] = jnp.zeros((SY, SZ), f32)
        faces[5][...] = jnp.zeros((SY, SZ), f32)

    def step(x, carry):
        centers, dxs, dys, dzs, laps = stencil(x, pad, halos[4], halos[5])
        diffs = dxs + dys + dzs
        for pair in range(2):
            operand = jnp.concatenate(
                [columns(diffs + [wall], 2 * pair), columns(diffs + [wall], 2 * pair + 1)], 1
            )
            for y in range(8):
                at = (pair * 8 + y) * WIDE
                pre = dot(first_w[y, 0:HID], operand)
                h_one_s[0:HID, at : at + WIDE] = jnp.tanh(pre.astype(bf16))
        for i in range(16):
            at = i * WIDE
            pre = dot(mid_w[...], h_one_s[:, at : at + WIDE])
            h_two_s[:, at : at + WIDE] = jnp.tanh(pre.astype(bf16))
        eddy = []
        for pair in range(2):
            logit = jnp.zeros((16, WIDE), f32)
            for y in range(8):
                at = (pair * 8 + y) * WIDE
                logit = logit + dot(out_w[y], h_two_s[:, at : at + WIDE])
            soft = eddy_scale * softplus(logit[:8])
            eddy += [soft[:, :SZ], soft[:, SZ:]]
        visc = base_viscosity + jnp.concatenate(eddy, 0)
        planes = []
        for c in range(3):
            advect = centers[0] * dxs[c] + centers[1] * dys[c] + centers[2] * dzs[c]
            moved = centers[c] + time_step * (visc * laps[c] - advect)
            if second:
                moved = 0.5 * velocity[c, x] + 0.5 * moved
            new[c, x] = moved
            planes.append(moved)
        if not second:
            put_faces(x, planes, *faces)
        return carry

    lax.fori_loop(0, SX, step, 0)
    if not second:
        faces[0][...] = new[:, 0]
        faces[1][...] = new[:, SX - 1]


def section(gy, v, halos, weights, velocity=None):
    second = velocity is not None
    outs = [jax.ShapeDtypeStruct((3, SX, SY, SZ), f32)]
    if not second:
        outs += face_structs()
    args = [gy, v, *halos] + ([velocity] if second else []) + list(weights)
    return pl.pallas_call(
        lambda *refs: section_kernel(second, *refs),
        out_shape=outs,
        in_specs=smem(1) + whole(len(args) - 1),
        out_specs=whole(len(outs)),
        scratch_shapes=[
            pltpu.VMEM((3, SX + 2, 48, SZ), f32),
            pltpu.VMEM((HID + 16, 16 * WIDE), bf16),
            pltpu.VMEM((HID, 16 * WIDE), bf16),
        ],
        name="section_two" if second else "section_one",
    )(*args)


def patch_kernel(
    gy, count, corner, dest, v, hx0, hx1, hy0, hy1, hz0, hz1, target,
    first_w, mid_w, out_w, mid_t, out_col, grads,
    tab, pad, feats, wall_s, tgt_s, h_one_s, h_two_s, d_one_s, d_two_s, f_s, d_s, row_s,
    acc_mid, acc_in, acc_out, stage,
):
    for t in range(TRAINERS):
        tab[3, t] = 0
    for s in range(SLOTS):
        d = dest[s]
        rank = tab[3, d]
        tab[3, d] = rank + 1
        spot = d * CAP + rank
        tab[0, spot] = corner[s, 1]
        tab[1, spot] = corner[s, 2]
        tab[2, spot] = jnp.where(s < count[0], 1, 0)
    wall_s[...] = wall_plane(gy[0])
    fill_padded(v, (hx0, hx1, hy0, hy1), pad)

    def plane(x, carry):
        _, dxs, dys, dzs, _ = stencil(x, pad, hz0, hz1)
        for i, diff in enumerate(dxs + dys + dzs):
            feats[i, x] = diff
        tgt_s[x] = target[x].astype(f32)
        return carry

    lax.fori_loop(0, SX, plane, 0)
    h_one_s[HID : HID + 16] = jnp.ones((16, 8 * WIDE), bf16)
    stage[...] = jnp.zeros((ROWS, SZ), f32)
    lane = lanes_of((PATCH, SZ))
    lane8 = lanes_of((8, WIDE))
    out_wide = out_col[...]

    def tile(i, carry):
        k = i // 4
        xo = i % 4

        @pl.when(xo == 0)
        def _():
            acc_mid[...] = jnp.zeros(acc_mid.shape, f32)
            acc_in[...] = jnp.zeros(acc_in.shape, f32)
            acc_out[...] = jnp.zeros(acc_out.shape, f32)

        chans = [jnp.zeros((PATCH, SZ), f32) for _ in range(11)]
        for q in range(8):
            xi, r = q // 2, q % 2
            spot = k * CAP + r
            cy, cz = tab[0, spot], tab[1, spot]
            x = xo * 4 + xi
            mine = lane // 16 == q
            turn = lax.rem(q * 16 - cz + SZ, SZ)
            for ch in range(11):
                if ch == 9:
                    piece = wall_s[pl.ds(cy, PATCH), :]
                elif ch == 10:
                    piece = tgt_s[x, pl.ds(cy, PATCH), :]
                else:
                    piece = feats[ch, x, pl.ds(cy, PATCH), :]
                if ch != 9:
                    piece = pltpu.roll(piece, turn, 1)
                chans[ch] = jnp.where(mine, piece, chans[ch])
        operand = jnp.concatenate([columns(chans[:10], 0), columns(chans[:10], 1)], 1)
        goal = jnp.concatenate([chans[10][:8], chans[10][8:]], 1)
        for y in range(8):
            at = y * WIDE
            pre = dot(first_w[y], operand)
            h_one_s[0:HID, at : at + WIDE] = jnp.tanh(pre[0:HID].astype(bf16))
            f_s[:, at : at + WIDE] = pre[HID : HID + 16].astype(bf16)
        for y in range(8):
            at = y * WIDE
            pre = dot(mid_w[...], h_one_s[:, at : at + WIDE])
            h_two_s[:, at : at + WIDE] = jnp.tanh(pre.astype(bf16))
        logit = jnp.zeros((16, WIDE), f32)
        for y in range(8):
            at = y * WIDE
            logit = logit + dot(out_w[y], h_two_s[:, at : at + WIDE])
        logit = logit[:8]
        live = jnp.where(
            (lane8 // 16) % 2 == 0, tab[2, k * CAP].astype(f32), tab[2, k * CAP + 1].astype(f32)
        )
        visc = eddy_scale * softplus(logit)
        delta = (live * (visc - goal) * eddy_scale * sigmoid(logit)).astype(bf16)
        row_s[...] = delta.astype(f32)
        for y in range(8):
            at = y * WIDE
            d_s[:, at : at + WIDE] = jnp.broadcast_to(row_s[y : y + 1], (16, WIDE)).astype(bf16)
            for half in range(2):
                to = at + half * SZ
                row = jnp.broadcast_to(row_s[y : y + 1, half * SZ : half * SZ + SZ], (HID, SZ))
                act = h_two_s[:, to : to + SZ].astype(f32)
                d_two_s[:, to : to + SZ] = (out_wide * row * (1.0 - act * act)).astype(bf16)
        acc_mid[...] += dot_nt(h_one_s[...], d_two_s[...])
        acc_out[...] += dot_nt(d_s[...], h_two_s[...])
        for y in range(8):
            at = y * WIDE
            back = dot(mid_t[...], d_two_s[:, at : at + WIDE])
            act = h_one_s[0:HID, at : at + WIDE].astype(f32)
            d_one_s[:, at : at + WIDE] = (back * (1.0 - act * act)).astype(bf16)
        acc_in[...] += dot_nt(f_s[...], d_one_s[...])

        @pl.when(xo == 3)
        def _():
            stage[0:HID] = acc_mid[0:HID]
            stage[HID : HID + 1] = acc_mid[HID : HID + 1]
            stage[HID + 1 : HID + 2] = acc_in[FEAT : FEAT + 1]
            stage[HID + 2 : HID + 3] = acc_out[0:1]
            stage[HID + 8 : HID + 8 + FEAT] = acc_in[0:FEAT]
            for q in range(4):
                grads[q, k] = stage[q * QROWS : (q + 1) * QROWS]

        return carry

    lax.fori_loop(0, 16, tile, 0)


def patch_grads(gy, count, corner, dest, v, halos, target, weights, mid_t, out_col):
    return pl.pallas_call(
        patch_kernel,
        out_shape=jax.ShapeDtypeStruct((4, TRAINERS, QROWS, SZ), f32),
        in_specs=smem(4) + whole(13),
        out_specs=pl.BlockSpec(memory_space=pltpu.VMEM),
        scratch_shapes=[
            pltpu.SMEM((4, 8), jnp.int32),
            pltpu.VMEM((3, SX + 2, 48, SZ), f32),
            pltpu.VMEM((9, SX, SY, SZ), f32),
            pltpu.VMEM((SY, SZ), f32),
            pltpu.VMEM((SX, SY, SZ), f32),
            pltpu.VMEM((HID + 16, 8 * WIDE), bf16),
            pltpu.VMEM((HID, 8 * WIDE), bf16),
            pltpu.VMEM((HID, 8 * WIDE), bf16),
            pltpu.VMEM((HID, 8 * WIDE), bf16),
            pltpu.VMEM((16, 8 * WIDE), bf16),
            pltpu.VMEM((16, 8 * WIDE), bf16),
            pltpu.VMEM((8, WIDE), f32),
            pltpu.VMEM((HID + 16, SZ), f32),
            pltpu.VMEM((16, SZ), f32),
            pltpu.VMEM((16, SZ), f32),
            pltpu.VMEM((ROWS, SZ), f32),
        ],
        name="patch_grads",
    )(gy, count, corner, dest, v, *halos, target, *weights, mid_t, out_col)


def gather_kernel(parts, out):
    total = parts[0]
    for i in range(1, 16):
        total = total + parts[i]
    square = jnp.sum(total * total)
    full = jnp.concatenate([total, jnp.zeros((SZ - QROWS, SZ), f32)], 0)
    out[...] = jnp.where(lanes_of((SZ, SZ)) == QROWS, square, full.T)


def scale_kernel(parts, out):
    x = parts[...].reshape(8, 2, 8, SZ)
    folded = x[:, 0] + x[:, 1]
    folded = folded.reshape(64, SZ)
    sub = sublanes_of((64, SZ))
    swapped = jnp.where(
        sub % 8 < 4, pltpu.roll(folded, 60, 0), pltpu.roll(folded, 4, 0)
    )
    norms = (folded + swapped)[:, QROWS : QROWS + 1]
    factor = jnp.broadcast_to(grad_gain / jnp.sqrt(norms + norm_epsilon), (64, SZ))
    scaled = x * factor.reshape(8, 1, 8, SZ)
    total = scaled[0]
    for i in range(1, 8):
        total = total + scaled[i]
    lane = lanes_of((1, SZ))
    quarters = []
    for q in range(4):
        rows = total[q // 2][(q % 2) * 4 : (q % 2) * 4 + 4]
        quarters.append(jnp.where(lane < QROWS, jnp.sum(rows, axis=0, keepdims=True), 0.0))
    left = quarters[0] + pltpu.roll(quarters[1], 40, 1) + pltpu.roll(quarters[2], 80, 1)
    tail = pltpu.roll(quarters[3], 120, 1)
    left = left + jnp.where(lane >= 120, tail, 0.0)
    right = jnp.where(lane < 32, tail, 0.0)
    out[...] = jnp.broadcast_to(jnp.concatenate([left, right], 1), (SZ, 2 * SZ))


def final_kernel(parts, mid, rest, rest_t):
    mid[...] = parts[:, 0:SZ]
    tail = parts[:, SZ : 2 * SZ]
    rest[...] = tail[:, 8 : 8 + FEAT]
    rest_t[...] = tail.T[0:8]


def call(kernel, outs, *args):
    return pl.pallas_call(
        kernel, out_shape=outs, in_specs=whole(len(args)),
        out_specs=jax.tree.map(lambda _: pl.BlockSpec(memory_space=pltpu.VMEM), outs),
        name=kernel.__name__,
    )(*args)


def struct(*shape):
    return jax.ShapeDtypeStruct(shape, f32)


def split_bias(bias):
    high = lax.reduce_precision(bias, 8, 7)
    middle = lax.reduce_precision(bias - high, 8, 7)
    low = bias - high - middle
    return jnp.stack([high, middle, low], 1).astype(bf16)


def prepare(weight_in, bias_in, weight_mid, bias_mid, weight_out):
    eye = jnp.eye(8, dtype=bf16)
    spread = (weight_in[None, :, :, None] * eye[:, None, None, :]).reshape(8, HID, FEAT * 8)
    bias = jnp.pad(split_bias(bias_in), ((0, 0), (0, 13)))
    first_w = jnp.concatenate([spread, jnp.broadcast_to(bias[None], (8, HID, 16))], 2)
    pick = jnp.eye(16, 11, dtype=bf16)[None, :, :, None] * jnp.concatenate(
        [jnp.broadcast_to(eye[:, None, None, :], (8, 1, FEAT, 8)),
         jnp.broadcast_to(eye[:1][:, None, None, :], (8, 1, 1, 8))], 2
    )
    pick = jnp.pad(pick.reshape(8, 16, 88), ((0, 0), (0, 0), (0, 8)))
    first_w = jnp.concatenate([first_w, pick], 1)
    mid_w = jnp.concatenate([weight_mid, jnp.pad(split_bias(bias_mid), ((0, 0), (0, 13)))], 1)
    out_w = jnp.pad(eye, ((0, 0), (0, 8)))[:, :, None] * weight_out[None, None, :]
    out_col = jnp.broadcast_to(weight_out.astype(f32)[:, None], (HID, SZ))
    return (first_w, mid_w, out_w), weight_mid.T, out_col


def on_device(
    velocity, target_visc, weight_in, bias_in, weight_mid, bias_mid, weight_out,
    patch_count, patch_corner, patch_dest,
):
    gy = lax.axis_index("gy").astype(jnp.int32).reshape(1)
    weights, mid_t, out_col = prepare(weight_in, bias_in, weight_mid, bias_mid, weight_out)
    halos = exchange(pack_faces(velocity))
    grads = patch_grads(
        gy, patch_count.reshape(1), patch_corner.reshape(SLOTS, 3), patch_dest.reshape(SLOTS),
        velocity, halos, target_visc, weights, mid_t, out_col,
    )
    every = ("gx", "gy", "gz")
    summed = lax.all_to_all(
        grads.reshape(16, QROWS, SZ), ("gy", "gz"), split_axis=0, concat_axis=0, tiled=True
    )
    velocity_late, grads = lax.optimization_barrier((velocity, grads))
    first, *faces = section(gy, velocity_late, halos, weights)
    summed, first = lax.optimization_barrier((summed, first))
    pieces = call(gather_kernel, struct(SZ, SZ), summed)
    pieces = lax.all_to_all(pieces, every, split_axis=0, concat_axis=0, tiled=True)
    halos = exchange(faces)
    pieces, halos = lax.optimization_barrier((pieces, halos))
    column = call(scale_kernel, struct(SZ, 2 * SZ), pieces)
    table = lax.all_to_all(column, every, split_axis=0, concat_axis=0, tiled=True)
    first, column = lax.optimization_barrier((first, column))
    (new_velocity,) = section(gy, first, halos, weights, velocity)
    table, new_velocity = lax.optimization_barrier((table, new_velocity))
    grad_mid, grad_in, rest = call(
        final_kernel, [struct(SZ, SZ), struct(SZ, FEAT), struct(8, SZ)], table
    )
    return (new_velocity, grad_in, rest[1], grad_mid, rest[0], rest[2])


def solution(mesh):
    in_specs = (
        P(None, "gx", "gy", "gz"),
        P("gx", "gy", "gz"),
        P(), P(), P(), P(), P(),
        P("gx", "gy", "gz"),
        P("gx", "gy", "gz", None, None),
        P("gx", "gy", "gz", None),
    )
    out_specs = (P(None, "gx", "gy", "gz"), P(), P(), P(), P(), P())
    return jax.shard_map(
        on_device, mesh=mesh, in_specs=in_specs, out_specs=out_specs, check_vma=False
    )
```

```python
import jax
import jax.numpy as jnp
from jax import lax
from jax.experimental import pallas as pl
from jax.experimental.pallas import tpu as pltpu
from jax.sharding import PartitionSpec as P

SX, SY, SZ = 16, 32, 128
HID = 128
FEAT = 10
PATCH = 16
CAP = 2
TRAINERS = 4
SLOTS = CAP * TRAINERS
ROWS = 160
QROWS = ROWS // 4
WIDE = 2 * SZ
GROUPS = 8
STAGES = ("output", "middle", "input", "forward")

time_step = 0.2
base_viscosity = 0.02
eddy_scale = 0.1
grad_gain = 20.0
norm_epsilon = 1e-06

f32 = jnp.float32
bf16 = jnp.bfloat16


def lanes_of(shape):
    return lax.broadcasted_iota(jnp.int32, shape, len(shape) - 1)


def sublanes_of(shape):
    return lax.broadcasted_iota(jnp.int32, shape, len(shape) - 2)


def softplus(x):
    return jnp.maximum(x, 0.0) + jnp.log1p(jnp.exp(-jnp.abs(x)))


def sigmoid(x):
    e = jnp.exp(-jnp.abs(x))
    return jnp.where(x >= 0, 1.0, e) / (1.0 + e)


def dot(a, b):
    return lax.dot_general(a, b, (((1,), (0,)), ((), ())), preferred_element_type=f32)


def dot_nt(a, b):
    return lax.dot_general(a, b, (((1,), (1,)), ((), ())), preferred_element_type=f32)


def wall_plane(gy):
    rows = (gy * SY + sublanes_of((SY, SZ))).astype(f32)
    return 1.0 - jnp.abs(2.0 * (rows + 0.5) / (SY * 4) - 1.0)


def put_faces(x, planes, xlo, xhi, ylo, yhi, zlo, zhi):
    lane = lanes_of((SY, SZ))
    low, high = zlo[...], zhi[...]
    for c in range(3):
        plane = planes[c]
        ylo[c, pl.ds(x, 1), :] = plane[0:1]
        yhi[c, pl.ds(x, 1), :] = plane[SY - 1 : SY]
        here = lane == c * SX + x
        low = jnp.where(here, jnp.broadcast_to(plane[:, 0:1], (SY, SZ)), low)
        high = jnp.where(here, jnp.broadcast_to(plane[:, SZ - 1 : SZ], (SY, SZ)), high)
    zlo[...] = low
    zhi[...] = high


def faces_kernel(v, xlo, xhi, ylo, yhi, zlo, zhi):
    zlo[...] = jnp.zeros((SY, SZ), f32)
    zhi[...] = jnp.zeros((SY, SZ), f32)
    xlo[...] = v[:, 0]
    xhi[...] = v[:, SX - 1]

    def step(x, carry):
        put_faces(x, [v[c, x] for c in range(3)], xlo, xhi, ylo, yhi, zlo, zhi)
        return carry

    lax.fori_loop(0, SX, step, 0)


FACE_SHAPES = ((3, SY, SZ),) * 2 + ((3, SX, SZ),) * 2 + ((SY, SZ),) * 2


def face_structs():
    return [jax.ShapeDtypeStruct(s, f32) for s in FACE_SHAPES]


def whole(n):
    return [pl.BlockSpec(memory_space=pltpu.VMEM) for _ in range(n)]


def smem(n):
    return [pl.BlockSpec(memory_space=pltpu.SMEM) for _ in range(n)]


def pack_faces(v):
    return pl.pallas_call(
        faces_kernel, out_shape=face_structs(), in_specs=whole(1), out_specs=whole(6), name="faces"
    )(v)


def exchange(faces):
    xlo, xhi, ylo, yhi, zlo, zhi = faces

    def shift(low, high, axis, closed):
        count = lax.axis_size(axis)
        ends = count if closed else count - 1
        from_low = lax.ppermute(high, axis, [(i, (i + 1) % count) for i in range(ends)])
        from_high = lax.ppermute(low, axis, [((i + 1) % count, i) for i in range(ends)])
        return from_low, from_high

    return (
        shift(xlo, xhi, "gx", True) + shift(ylo, yhi, "gy", False) + shift(zlo, zhi, "gz", True)
    )


def fill_padded(v, halos, pad):
    hx0, hx1, hy0, hy1 = halos[:4]
    for c in range(3):
        pad[c, 0, 8 : 8 + SY] = hx0[c]
        pad[c, SX + 1, 8 : 8 + SY] = hx1[c]

    def step(x, carry):
        for c in range(3):
            pad[c, x + 1, 8 : 8 + SY] = v[c, x]
            pad[c, x + 1, 7:8] = hy0[c, pl.ds(x, 1), :]
            pad[c, x + 1, 8 + SY : 9 + SY] = hy1[c, pl.ds(x, 1), :]
        return carry

    lax.fori_loop(0, SX, step, 0)


def stencil(x, pad, hz0, hz1):
    lane = lanes_of((SY, SZ))
    low, high = hz0[...], hz1[...]
    centers, dxs, dys, dzs, laps = [], [], [], [], []
    for c in range(3):
        at = c * SX + x
        ctr = pad[c, x + 1, 8 : 8 + SY]
        xm, xp = pad[c, x, 8 : 8 + SY], pad[c, x + 2, 8 : 8 + SY]
        ym, yp = pad[c, x + 1, 7 : 7 + SY], pad[c, x + 1, 9 : 9 + SY]
        zm = jnp.where(lane == 0, pltpu.roll(low, (SZ - at) % SZ, 1), pltpu.roll(ctr, 1, 1))
        zp = jnp.where(
            lane == SZ - 1, pltpu.roll(high, SZ - 1 - at, 1), pltpu.roll(ctr, SZ - 1, 1)
        )
        centers.append(ctr)
        dxs.append((xp - xm) * 0.5)
        dys.append((yp - ym) * 0.5)
        dzs.append((zp - zm) * 0.5)
        laps.append(xp + xm + yp + ym + zp + zm - 6.0 * ctr)
    return centers, dxs, dys, dzs, laps


def columns(channels, group):
    parts = [ch[group * 8 : group * 8 + 8] for ch in channels]
    parts.append(jnp.ones((16, SZ), f32))
    return jnp.concatenate(parts, 0).astype(bf16)


def section_kernel(second, *refs):
    gy = refs[0]
    v, *halos = refs[1:8]
    at = 8
    if second:
        velocity = refs[at]
        at += 1
    first_w, mid_w, out_col = refs[at : at + 3]
    at += 3
    new = refs[at]
    at += 1
    if not second:
        faces = refs[at : at + 6]
        at += 6
    pad, op_s, h_one_s, logit_s, adv_s, lap_s = refs[at : at + 6]
    fill_padded(v, halos, pad)
    wall = wall_plane(gy[0])
    h_one_s[HID : HID + 16] = jnp.ones((16, 16 * WIDE), bf16)
    if not second:
        faces[4][...] = jnp.zeros((SY, SZ), f32)
        faces[5][...] = jnp.zeros((SY, SZ), f32)

    def begin(x):
        centers, dxs, dys, dzs, laps = stencil(x, pad, halos[4], halos[5])
        chans = dxs + dys + dzs + [wall]
        for group in range(4):
            op_s[:, group * SZ : group * SZ + SZ] = columns(chans, group)
        slot = x % 4
        for c in range(3):
            adv_s[slot, c] = centers[0] * dxs[c] + centers[1] * dys[c] + centers[2] * dzs[c]
            lap_s[slot, c] = laps[c]

    def finish(x, slot):
        visc = base_viscosity + eddy_scale * softplus(logit_s[...])
        planes = []
        for c in range(3):
            rate = visc * lap_s[slot, c] - adv_s[slot, c]
            moved = pad[c, x + 1, 8 : 8 + SY] + time_step * rate
            if second:
                moved = 0.5 * velocity[c, x] + 0.5 * moved
            new[c, x] = moved
            planes.append(moved)
        if not second:
            put_faces(x, planes, *faces)

    def layer_one(i):
        operand = op_s[:, i // 8 * WIDE : i // 8 * WIDE + WIDE]
        pre = dot(first_w[i % 8, 0:HID], operand)
        h_one_s[0:HID, i * WIDE : i * WIDE + WIDE] = jnp.tanh(pre.astype(bf16))

    def layer_two(i):
        pre = dot(mid_w[...], h_one_s[:, i * WIDE : i * WIDE + WIDE])
        h_two = jnp.tanh(pre.astype(bf16)).astype(f32)
        for half in range(2):
            to = ((i // 8) * 2 + half) * 8 + i % 8
            terms = h_two[:, half * SZ : half * SZ + SZ] * out_col[...]
            logit_s[to : to + 1] = jnp.sum(terms, axis=0, keepdims=True)

    begin(0)
    for i in range(16):
        layer_one(i)
    begin(1)

    def step(x, carry):
        finish(jnp.maximum(x - 1, 0), (x + 3) % 4)
        for i in range(16):
            layer_two(i)
            layer_one(i)
        begin(jnp.minimum(x + 2, SX - 1))
        return carry

    lax.fori_loop(0, SX, step, 0)
    finish(SX - 1, (SX - 1) % 4)
    if not second:
        faces[0][...] = new[:, 0]
        faces[1][...] = new[:, SX - 1]


def section(gy, v, halos, weights, velocity=None):
    second = velocity is not None
    outs = [jax.ShapeDtypeStruct((3, SX, SY, SZ), f32)]
    if not second:
        outs += face_structs()
    args = [gy, v, *halos] + ([velocity] if second else []) + list(weights)
    return pl.pallas_call(
        lambda *refs: section_kernel(second, *refs),
        out_shape=outs,
        in_specs=smem(1) + whole(len(args) - 1),
        out_specs=whole(len(outs)),
        scratch_shapes=[
            pltpu.VMEM((3, SX + 2, 48, SZ), f32),
            pltpu.VMEM((96, 4 * SZ), bf16),
            pltpu.VMEM((HID + 16, 16 * WIDE), bf16),
            pltpu.VMEM((SY, SZ), f32),
            pltpu.VMEM((4, 3, SY, SZ), f32),
            pltpu.VMEM((4, 3, SY, SZ), f32),
        ],
        name="section_two" if second else "section_one",
    )(*args)


def patch_kernel(
    gy, count, corner, dest, v, hx0, hx1, hy0, hy1, hz0, hz1, target,
    first_w, mid_w, out_w, mid_t, out_col, grads,
    tab, pad, feats, wall_s, tgt_s, op_s, goal_s, h_one_s, h_two_s, d_one_s, d_two_s, f_s, d_s, row_s,
    acc_mid, acc_in, acc_out, stage,
):
    for t in range(TRAINERS):
        tab[3, t] = 0
    for s in range(SLOTS):
        d = dest[s]
        rank = tab[3, d]
        tab[3, d] = rank + 1
        spot = d * CAP + rank
        tab[0, spot] = corner[s, 1]
        tab[1, spot] = corner[s, 2]
        tab[2, spot] = jnp.where(s < count[0], 1, 0)
    wall_s[...] = wall_plane(gy[0])
    fill_padded(v, (hx0, hx1, hy0, hy1), pad)

    def plane(x, carry):
        _, dxs, dys, dzs, _ = stencil(x, pad, hz0, hz1)
        for i, diff in enumerate(dxs + dys + dzs):
            feats[i, x] = diff
        tgt_s[x] = target[x].astype(f32)
        return carry

    lax.fori_loop(0, SX, plane, 0)
    h_one_s[HID : HID + 16] = jnp.ones((16, 8 * WIDE), bf16)
    stage[...] = jnp.zeros((ROWS, SZ), f32)
    lane = lanes_of((PATCH, SZ))
    lane8 = lanes_of((8, WIDE))
    out_wide = out_col[...]

    def assemble(i):
        k = i // 4
        xo = i % 4
        chans = [jnp.zeros((PATCH, SZ), f32) for _ in range(11)]
        for q in range(8):
            xi, r = q // 2, q % 2
            spot = k * CAP + r
            cy, cz = tab[0, spot], tab[1, spot]
            x = xo * 4 + xi
            mine = lane // 16 == q
            turn = lax.rem(q * 16 - cz + SZ, SZ)
            for ch in range(11):
                if ch == 9:
                    piece = wall_s[pl.ds(cy, PATCH), :]
                elif ch == 10:
                    piece = tgt_s[x, pl.ds(cy, PATCH), :]
                else:
                    piece = feats[ch, x, pl.ds(cy, PATCH), :]
                if ch != 9:
                    piece = pltpu.roll(piece, turn, 1)
                chans[ch] = jnp.where(mine, piece, chans[ch])
        for half in range(2):
            op_s[:, half * SZ : half * SZ + SZ] = columns(chans[:10], half)
            goal_s[:, half * SZ : half * SZ + SZ] = chans[10][half * 8 : half * 8 + 8]

    def layer_one(y):
        at = y * WIDE
        pre = dot(first_w[y], op_s[...])
        h_one_s[0:HID, at : at + WIDE] = jnp.tanh(pre[0:HID].astype(bf16))
        f_s[:, at : at + WIDE] = pre[HID : HID + 16].astype(bf16)

    def layer_two(y):
        at = y * WIDE
        pre = dot(mid_w[...], h_one_s[:, at : at + WIDE])
        h_two = jnp.tanh(pre.astype(bf16))
        h_two_s[:, at : at + WIDE] = h_two
        return dot(out_w[y], h_two)

    def errors(k, logit):
        live = jnp.where(
            (lane8 // 16) % 2 == 0, tab[2, k * CAP].astype(f32), tab[2, k * CAP + 1].astype(f32)
        )
        visc = eddy_scale * softplus(logit)
        delta = live * (visc - goal_s[...]) * eddy_scale * sigmoid(logit)
        row_s[...] = delta.astype(bf16).astype(f32)

    def output_side(y):
        at = y * WIDE
        d_s[:, at : at + WIDE] = jnp.broadcast_to(row_s[y : y + 1], (16, WIDE)).astype(bf16)
        for half in range(2):
            to = at + half * SZ
            row = jnp.broadcast_to(row_s[y : y + 1, half * SZ : half * SZ + SZ], (HID, SZ))
            act = h_two_s[:, to : to + SZ].astype(f32)
            d_two_s[:, to : to + SZ] = (out_wide * row * (1.0 - act * act)).astype(bf16)

    def input_side(y):
        at = y * WIDE
        back = dot(mid_t[...], d_two_s[:, at : at + WIDE])
        act = h_one_s[0:HID, at : at + WIDE].astype(f32)
        d_one_s[:, at : at + WIDE] = (back * (1.0 - act * act)).astype(bf16)

    def add_output(ys):
        span = slice(ys[0] * WIDE, (ys[-1] + 1) * WIDE)
        acc_mid[...] += dot_nt(h_one_s[:, span], d_two_s[:, span])
        acc_out[...] += dot_nt(d_s[:, span], h_two_s[:, span])

    def add_input(ys):
        span = slice(ys[0] * WIDE, (ys[-1] + 1) * WIDE)
        acc_in[...] += dot_nt(f_s[:, span], d_one_s[:, span])

    assemble(0)
    for y in range(8):
        layer_one(y)
    logit = jnp.zeros((16, WIDE), f32)
    for y in range(8):
        logit = logit + layer_two(y)
    errors(0, logit[:8])
    assemble(1)

    def tile(i, carry):
        @pl.when(i % 4 == 0)
        def _():
            acc_mid[...] = jnp.zeros(acc_mid.shape, f32)
            acc_in[...] = jnp.zeros(acc_in.shape, f32)
            acc_out[...] = jnp.zeros(acc_out.shape, f32)

        logit = jnp.zeros((16, WIDE), f32)
        size = 8 // GROUPS
        for step in range(GROUPS + 4):
            for stage_at, work in enumerate(STAGES):
                group = step - stage_at
                if not 0 <= group < GROUPS:
                    continue
                ys = [group * size + j for j in range(size)]
                if work == "output":
                    for y in ys:
                        output_side(y)
                elif work == "middle":
                    for y in ys:
                        input_side(y)
                    add_output(ys)
                elif work == "input":
                    add_input(ys)
                    for y in ys:
                        layer_one(y)
                else:
                    for y in ys:
                        logit = logit + layer_two(y)
        errors(jnp.minimum(i + 1, 15) // 4, logit[:8])
        assemble(jnp.minimum(i + 2, 15))

        @pl.when(i % 4 == 3)
        def _():
            k = i // 4
            stage[0:HID] = acc_mid[0:HID]
            stage[HID : HID + 1] = acc_mid[HID : HID + 1]
            stage[HID + 1 : HID + 2] = acc_in[FEAT : FEAT + 1]
            stage[HID + 2 : HID + 3] = acc_out[0:1]
            stage[HID + 8 : HID + 8 + FEAT] = acc_in[0:FEAT]
            for q in range(4):
                grads[q, k] = stage[q * QROWS : (q + 1) * QROWS]

        return carry

    lax.fori_loop(0, 16, tile, 0)


def patch_grads(gy, count, corner, dest, v, halos, target, weights, mid_t, out_col):
    return pl.pallas_call(
        patch_kernel,
        out_shape=jax.ShapeDtypeStruct((4, TRAINERS, QROWS, SZ), f32),
        in_specs=smem(4) + whole(13),
        out_specs=pl.BlockSpec(memory_space=pltpu.VMEM),
        scratch_shapes=[
            pltpu.SMEM((4, 8), jnp.int32),
            pltpu.VMEM((3, SX + 2, 48, SZ), f32),
            pltpu.VMEM((9, SX, SY, SZ), f32),
            pltpu.VMEM((SY, SZ), f32),
            pltpu.VMEM((SX, SY, SZ), f32),
            pltpu.VMEM((96, WIDE), bf16),
            pltpu.VMEM((8, WIDE), f32),
            pltpu.VMEM((HID + 16, 8 * WIDE), bf16),
            pltpu.VMEM((HID, 8 * WIDE), bf16),
            pltpu.VMEM((HID, 8 * WIDE), bf16),
            pltpu.VMEM((HID, 8 * WIDE), bf16),
            pltpu.VMEM((16, 8 * WIDE), bf16),
            pltpu.VMEM((16, 8 * WIDE), bf16),
            pltpu.VMEM((8, WIDE), f32),
            pltpu.VMEM((HID + 16, SZ), f32),
            pltpu.VMEM((16, SZ), f32),
            pltpu.VMEM((16, SZ), f32),
            pltpu.VMEM((ROWS, SZ), f32),
        ],
        name="patch_grads",
    )(gy, count, corner, dest, v, *halos, target, *weights, mid_t, out_col)


def gather_kernel(parts, out):
    total = parts[0]
    for i in range(1, 16):
        total = total + parts[i]
    square = jnp.sum(total * total)
    full = jnp.concatenate([total, jnp.zeros((SZ - QROWS, SZ), f32)], 0)
    out[...] = jnp.where(lanes_of((SZ, SZ)) == QROWS, square, full.T)


def scale_kernel(parts, out):
    x = parts[...].reshape(8, 2, 8, SZ)
    folded = x[:, 0] + x[:, 1]
    folded = folded.reshape(64, SZ)
    sub = sublanes_of((64, SZ))
    swapped = jnp.where(
        sub % 8 < 4, pltpu.roll(folded, 60, 0), pltpu.roll(folded, 4, 0)
    )
    norms = (folded + swapped)[:, QROWS : QROWS + 1]
    factor = jnp.broadcast_to(grad_gain / jnp.sqrt(norms + norm_epsilon), (64, SZ))
    scaled = x * factor.reshape(8, 1, 8, SZ)
    total = scaled[0]
    for i in range(1, 8):
        total = total + scaled[i]
    lane = lanes_of((1, SZ))
    quarters = []
    for q in range(4):
        rows = total[q // 2][(q % 2) * 4 : (q % 2) * 4 + 4]
        quarters.append(jnp.where(lane < QROWS, jnp.sum(rows, axis=0, keepdims=True), 0.0))
    left = quarters[0] + pltpu.roll(quarters[1], 40, 1) + pltpu.roll(quarters[2], 80, 1)
    tail = pltpu.roll(quarters[3], 120, 1)
    left = left + jnp.where(lane >= 120, tail, 0.0)
    right = jnp.where(lane < 32, tail, 0.0)
    row = jnp.concatenate([left, right], 1)
    out[...] = jnp.broadcast_to(row.reshape(1, 1, 2 * SZ), (SZ, 1, 2 * SZ))


def final_kernel(parts, mid, rest_in, bias_in, bias_mid, rest_out):
    mid[...] = parts[:, 0:SZ]
    tail = parts[:, SZ : 2 * SZ].T
    bias_mid[...] = tail[0:1]
    bias_in[...] = tail[1:2]
    rest_out[...] = tail[2:3]
    rest_in[...] = tail[8 : 8 + FEAT]


def call(kernel, outs, *args):
    return pl.pallas_call(
        kernel, out_shape=outs, in_specs=whole(len(args)),
        out_specs=jax.tree.map(lambda _: pl.BlockSpec(memory_space=pltpu.VMEM), outs),
        name=kernel.__name__,
    )(*args)


def struct(*shape):
    return jax.ShapeDtypeStruct(shape, f32)


def bias_rows(bias):
    high = bias.astype(bf16).astype(f32)
    middle = (bias - high).astype(bf16).astype(f32)
    low = bias - high - middle
    sub = sublanes_of((16, HID))
    rows = jnp.where(sub == 0, high, jnp.where(sub == 1, middle, jnp.where(sub == 2, low, 0.0)))
    return rows.astype(bf16)


def one_hot(shape, test):
    return jnp.where(test(sublanes_of(shape), lanes_of(shape)), 1.0, 0.0).astype(bf16)


def prepare_kernel(w_in, b_in, w_mid, b_mid, w_out, first_w, mid_w, mid_t, out_w, out_col):
    eye = one_hot((HID, HID), lambda i, j: i == j)
    bias = dot_nt(eye, bias_rows(b_in[...])).astype(bf16)
    bias_part = dot(bias, one_hot((16, 96), lambda i, j: j == 80 + i))
    row = jnp.broadcast_to(w_out[...], (16, HID))
    sub = sublanes_of((16, HID))
    for y in range(8):
        spread = one_hot((FEAT, 96), lambda i, j: j == i * 8 + y)
        first_w[y, 0:HID] = (dot(w_in[...], spread) + bias_part).astype(bf16)
        first_w[y, HID : HID + 16] = one_hot(
            (16, 96),
            lambda i, j: ((i < FEAT) & (j == i * 8 + y)) | ((i == FEAT) & (j == FEAT * 8)),
        )
        out_w[y] = jnp.where(sub == y, row.astype(f32), 0.0).astype(bf16)
    mid_w[:, 0:HID] = w_mid[...]
    mid_w[:, HID : HID + 16] = dot_nt(eye, bias_rows(b_mid[...])).astype(bf16)
    mid_t[...] = dot_nt(eye, w_mid[...]).astype(bf16)
    out_col[...] = dot_nt(eye, jnp.broadcast_to(w_out[...], (HID, HID)))


def prepare(weight_in, bias_in, weight_mid, bias_mid, weight_out):
    outs = [
        jax.ShapeDtypeStruct((8, HID + 16, 96), bf16),
        jax.ShapeDtypeStruct((HID, HID + 16), bf16),
        jax.ShapeDtypeStruct((HID, HID), bf16),
        jax.ShapeDtypeStruct((8, 16, HID), bf16),
        struct(HID, SZ),
    ]
    return call(
        prepare_kernel, outs, weight_in, bias_in.reshape(1, HID), weight_mid,
        bias_mid.reshape(1, HID), weight_out.reshape(1, HID),
    )


def on_device(
    velocity, target_visc, weight_in, bias_in, weight_mid, bias_mid, weight_out,
    patch_count, patch_corner, patch_dest,
):
    gy = lax.axis_index("gy").astype(jnp.int32).reshape(1)
    first_w, mid_w, mid_t, out_w, out_col = prepare(
        weight_in, bias_in, weight_mid, bias_mid, weight_out
    )
    net = (first_w, mid_w, out_col)
    halos = exchange(pack_faces(velocity))
    grads = patch_grads(
        gy, patch_count.reshape(1), patch_corner.reshape(SLOTS, 3), patch_dest.reshape(SLOTS),
        velocity, halos, target_visc, (first_w, mid_w, out_w), mid_t, out_col,
    )
    every = ("gx", "gy", "gz")
    summed = lax.all_to_all(
        grads.reshape(16, QROWS, SZ), ("gy", "gz"), split_axis=0, concat_axis=0, tiled=True
    )
    velocity_late, grads = lax.optimization_barrier((velocity, grads))
    first, *faces = section(gy, velocity_late, halos, net)
    summed, first = lax.optimization_barrier((summed, first))
    pieces = call(gather_kernel, struct(SZ, SZ), summed)
    pieces = lax.all_to_all(pieces, every, split_axis=0, concat_axis=0, tiled=True)
    halos = exchange(faces)
    pieces, halos = lax.optimization_barrier((pieces, halos))
    column = call(scale_kernel, struct(SZ, 1, 2 * SZ), pieces)
    table = lax.all_to_all(column, every, split_axis=0, concat_axis=0, tiled=True)
    first, column = lax.optimization_barrier((first, column))
    (new_velocity,) = section(gy, first, halos, net, velocity)
    table, new_velocity = lax.optimization_barrier((table, new_velocity))
    grad_mid, grad_in, grad_b_in, grad_b_mid, grad_out = call(
        final_kernel,
        [struct(HID, HID), struct(FEAT, HID), struct(1, HID), struct(1, HID), struct(1, HID)],
        table.reshape(SZ, 2 * SZ),
    )
    return (
        new_velocity, grad_in.T, grad_b_in.reshape(HID), grad_mid, grad_b_mid.reshape(HID),
        grad_out.reshape(HID),
    )


def solution(mesh):
    in_specs = (
        P(None, "gx", "gy", "gz"),
        P("gx", "gy", "gz"),
        P(), P(), P(), P(), P(),
        P("gx", "gy", "gz"),
        P("gx", "gy", "gz", None, None),
        P("gx", "gy", "gz", None),
    )
    out_specs = (P(None, "gx", "gy", "gz"), P(), P(), P(), P(), P())
    return jax.shard_map(
        on_device, mesh=mesh, in_specs=in_specs, out_specs=out_specs, check_vma=False
    )
```

```python
import jax
import jax.numpy as jnp
from jax import lax
from jax.experimental import pallas as pl
from jax.experimental.pallas import tpu as pltpu
from jax.sharding import PartitionSpec as P

SX, SY, SZ = 16, 32, 128
HID = 128
FEAT = 10
PATCH = 16
CAP = 2
TRAINERS = 4
SLOTS = CAP * TRAINERS
ROWS = 160
QROWS = ROWS // 4
WIDE = 2 * SZ
LAGS = (0, 1, 2, 3, 5)

time_step = 0.2
base_viscosity = 0.02
eddy_scale = 0.1
grad_gain = 20.0
norm_epsilon = 1e-06

f32 = jnp.float32
bf16 = jnp.bfloat16


def lanes_of(shape):
    return lax.broadcasted_iota(jnp.int32, shape, len(shape) - 1)


def sublanes_of(shape):
    return lax.broadcasted_iota(jnp.int32, shape, len(shape) - 2)


def softplus(x):
    return jnp.maximum(x, 0.0) + jnp.log1p(jnp.exp(-jnp.abs(x)))


def sigmoid(x):
    e = jnp.exp(-jnp.abs(x))
    return jnp.where(x >= 0, 1.0, e) / (1.0 + e)


def dot(a, b):
    return lax.dot_general(a, b, (((1,), (0,)), ((), ())), preferred_element_type=f32)


def dot_nt(a, b):
    return lax.dot_general(a, b, (((1,), (1,)), ((), ())), preferred_element_type=f32)


def wall_plane(gy):
    rows = (gy * SY + sublanes_of((SY, SZ))).astype(f32)
    return 1.0 - jnp.abs(2.0 * (rows + 0.5) / (SY * 4) - 1.0)


def put_faces(x, planes, xlo, xhi, ylo, yhi, zlo, zhi):
    lane = lanes_of((SY, SZ))
    low, high = zlo[...], zhi[...]
    for c in range(3):
        plane = planes[c]
        ylo[c, pl.ds(x, 1), :] = plane[0:1]
        yhi[c, pl.ds(x, 1), :] = plane[SY - 1 : SY]
        here = lane == c * SX + x
        low = jnp.where(here, jnp.broadcast_to(plane[:, 0:1], (SY, SZ)), low)
        high = jnp.where(here, jnp.broadcast_to(plane[:, SZ - 1 : SZ], (SY, SZ)), high)
    zlo[...] = low
    zhi[...] = high


def faces_kernel(v, xlo, xhi, ylo, yhi, zlo, zhi):
    zlo[...] = jnp.zeros((SY, SZ), f32)
    zhi[...] = jnp.zeros((SY, SZ), f32)
    xlo[...] = v[:, 0]
    xhi[...] = v[:, SX - 1]

    def step(i, carry):
        for x in [i * 4 + j for j in range(4)]:
            put_faces(x, [v[c, x] for c in range(3)], xlo, xhi, ylo, yhi, zlo, zhi)
        return carry

    lax.fori_loop(0, SX // 4, step, 0)


FACE_SHAPES = ((3, SY, SZ),) * 2 + ((3, SX, SZ),) * 2 + ((SY, SZ),) * 2


def face_structs():
    return [jax.ShapeDtypeStruct(s, f32) for s in FACE_SHAPES]


def whole(n):
    return [pl.BlockSpec(memory_space=pltpu.VMEM) for _ in range(n)]


def smem(n):
    return [pl.BlockSpec(memory_space=pltpu.SMEM) for _ in range(n)]


def pack_faces(v):
    return pl.pallas_call(
        faces_kernel, out_shape=face_structs(), in_specs=whole(1), out_specs=whole(6), name="faces"
    )(v)


def exchange(faces):
    xlo, xhi, ylo, yhi, zlo, zhi = faces

    def shift(low, high, axis, closed):
        count = lax.axis_size(axis)
        ends = count if closed else count - 1
        from_low = lax.ppermute(high, axis, [(i, (i + 1) % count) for i in range(ends)])
        from_high = lax.ppermute(low, axis, [((i + 1) % count, i) for i in range(ends)])
        return from_low, from_high

    return (
        shift(xlo, xhi, "gx", True) + shift(ylo, yhi, "gy", False) + shift(zlo, zhi, "gz", True)
    )


def fill_padded(v, halos, pad):
    hx0, hx1, hy0, hy1 = halos[:4]
    for c in range(3):
        pad[c, 0, 8 : 8 + SY] = hx0[c]
        pad[c, SX + 1, 8 : 8 + SY] = hx1[c]

    def step(i, carry):
        for x in [i * 4 + j for j in range(4)]:
            for c in range(3):
                pad[c, x + 1, 8 : 8 + SY] = v[c, x]
                pad[c, x + 1, 7:8] = hy0[c, pl.ds(x, 1), :]
                pad[c, x + 1, 8 + SY : 9 + SY] = hy1[c, pl.ds(x, 1), :]
        return carry

    lax.fori_loop(0, SX // 4, step, 0)


def stencil(x, pad, hz0, hz1):
    lane = lanes_of((SY, SZ))
    low, high = hz0[...], hz1[...]
    centers, dxs, dys, dzs, laps = [], [], [], [], []
    for c in range(3):
        at = c * SX + x
        ctr = pad[c, x + 1, 8 : 8 + SY]
        xm, xp = pad[c, x, 8 : 8 + SY], pad[c, x + 2, 8 : 8 + SY]
        ym, yp = pad[c, x + 1, 7 : 7 + SY], pad[c, x + 1, 9 : 9 + SY]
        zm = jnp.where(lane == 0, pltpu.roll(low, (SZ - at) % SZ, 1), pltpu.roll(ctr, 1, 1))
        zp = jnp.where(
            lane == SZ - 1, pltpu.roll(high, SZ - 1 - at, 1), pltpu.roll(ctr, SZ - 1, 1)
        )
        centers.append(ctr)
        dxs.append((xp - xm) * 0.5)
        dys.append((yp - ym) * 0.5)
        dzs.append((zp - zm) * 0.5)
        laps.append(xp + xm + yp + ym + zp + zm - 6.0 * ctr)
    return centers, dxs, dys, dzs, laps


def columns(channels, group):
    parts = [ch[group * 8 : group * 8 + 8] for ch in channels]
    parts.append(jnp.ones((16, SZ), f32))
    return jnp.concatenate(parts, 0).astype(bf16)


def section_kernel(second, *refs):
    gy = refs[0]
    v, *halos = refs[1:8]
    at = 8
    if second:
        velocity = refs[at]
        at += 1
    first_w, mid_w, out_col = refs[at : at + 3]
    at += 3
    new = refs[at]
    at += 1
    if not second:
        faces = refs[at : at + 6]
        at += 6
    pad, op_s, h_one_s, logit_s, adv_s, lap_s = refs[at : at + 6]
    fill_padded(v, halos, pad)
    wall = wall_plane(gy[0])
    h_one_s[HID : HID + 16] = jnp.ones((16, 16 * WIDE), bf16)
    if not second:
        faces[4][...] = jnp.zeros((SY, SZ), f32)
        faces[5][...] = jnp.zeros((SY, SZ), f32)

    def begin(x):
        centers, dxs, dys, dzs, laps = stencil(x, pad, halos[4], halos[5])
        chans = dxs + dys + dzs + [wall]
        for group in range(4):
            op_s[:, group * SZ : group * SZ + SZ] = columns(chans, group)
        slot = x % 4
        for c in range(3):
            adv_s[slot, c] = centers[0] * dxs[c] + centers[1] * dys[c] + centers[2] * dzs[c]
            lap_s[slot, c] = laps[c]

    def finish(x, slot):
        visc = base_viscosity + eddy_scale * softplus(logit_s[...])
        planes = []
        for c in range(3):
            rate = visc * lap_s[slot, c] - adv_s[slot, c]
            moved = pad[c, x + 1, 8 : 8 + SY] + time_step * rate
            if second:
                moved = 0.5 * velocity[c, x] + 0.5 * moved
            new[c, x] = moved
            planes.append(moved)
        if not second:
            put_faces(x, planes, *faces)

    def layer_one(i):
        operand = op_s[:, i // 8 * WIDE : i // 8 * WIDE + WIDE]
        pre = dot(first_w[i % 8, 0:HID], operand)
        h_one_s[0:HID, i * WIDE : i * WIDE + WIDE] = jnp.tanh(pre.astype(bf16))

    def layer_two(i):
        pre = dot(mid_w[...], h_one_s[:, i * WIDE : i * WIDE + WIDE])
        h_two = jnp.tanh(pre.astype(bf16)).astype(f32)
        for half in range(2):
            to = ((i // 8) * 2 + half) * 8 + i % 8
            terms = h_two[:, half * SZ : half * SZ + SZ] * out_col[...]
            logit_s[to : to + 1] = jnp.sum(terms, axis=0, keepdims=True)

    begin(0)
    for i in range(16):
        layer_one(i)
    begin(1)

    def step(x, carry):
        finish(jnp.maximum(x - 1, 0), (x + 3) % 4)
        for i in range(16):
            layer_two(i)
            layer_one(i)
        begin(jnp.minimum(x + 2, SX - 1))
        return carry

    lax.fori_loop(0, SX, step, 0)
    finish(SX - 1, (SX - 1) % 4)
    if not second:
        faces[0][...] = new[:, 0]
        faces[1][...] = new[:, SX - 1]


def section(gy, v, halos, weights, velocity=None):
    second = velocity is not None
    outs = [jax.ShapeDtypeStruct((3, SX, SY, SZ), f32)]
    if not second:
        outs += face_structs()
    args = [gy, v, *halos] + ([velocity] if second else []) + list(weights)
    return pl.pallas_call(
        lambda *refs: section_kernel(second, *refs),
        out_shape=outs,
        in_specs=smem(1) + whole(len(args) - 1),
        out_specs=whole(len(outs)),
        scratch_shapes=[
            pltpu.VMEM((3, SX + 2, 48, SZ), f32),
            pltpu.VMEM((96, 4 * SZ), bf16),
            pltpu.VMEM((HID + 16, 16 * WIDE), bf16),
            pltpu.VMEM((SY, SZ), f32),
            pltpu.VMEM((4, 3, SY, SZ), f32),
            pltpu.VMEM((4, 3, SY, SZ), f32),
        ],
        name="section_two" if second else "section_one",
    )(*args)


def patch_kernel(
    gy, count, corner, dest, v, hx0, hx1, hy0, hy1, hz0, hz1, target,
    first_w, mid_w, out_w, mid_t, out_col, grads,
    tab, pad, feats, wall_s, tgt_s, chan_s, op_s, goal_s, h_one_s, h_two_s, d_one_s, d_two_s, f_s, d_s, row_s,
    acc_mid, acc_in, acc_out, stage,
):
    for t in range(TRAINERS):
        tab[3, t] = 0
    for s in range(SLOTS):
        d = dest[s]
        rank = tab[3, d]
        tab[3, d] = rank + 1
        spot = d * CAP + rank
        tab[0, spot] = corner[1, s]
        tab[1, spot] = corner[2, s]
        tab[2, spot] = jnp.where(s < count[0], 1, 0)
    wall_s[...] = wall_plane(gy[0])
    fill_padded(v, (hx0, hx1, hy0, hy1), pad)

    def plane(i, carry):
        for x in [i * 2, i * 2 + 1]:
            _, dxs, dys, dzs, _ = stencil(x, pad, hz0, hz1)
            for f, diff in enumerate(dxs + dys + dzs):
                feats[f, x] = diff
            tgt_s[x] = target[x].astype(f32)
        return carry

    lax.fori_loop(0, SX // 2, plane, 0)
    h_one_s[HID : HID + 16] = jnp.ones((16, 8 * WIDE), bf16)
    stage[...] = jnp.zeros((ROWS, SZ), f32)
    lane = lanes_of((PATCH, SZ))
    lane8 = lanes_of((8, WIDE))
    out_wide = out_col[...]

    def assemble(i):
        k = i // 4
        xo = i % 4
        chans = [jnp.zeros((PATCH, SZ), f32) for _ in range(11)]
        for q in range(8):
            xi, r = q // 2, q % 2
            spot = k * CAP + r
            cy, cz = tab[0, spot], tab[1, spot]
            x = xo * 4 + xi
            mine = lane // 16 == q
            turn = lax.rem(q * 16 - cz + SZ, SZ)
            for ch in range(11):
                if ch == 9:
                    piece = wall_s[pl.ds(cy, PATCH), :]
                elif ch == 10:
                    piece = tgt_s[x, pl.ds(cy, PATCH), :]
                else:
                    piece = feats[ch, x, pl.ds(cy, PATCH), :]
                if ch != 9:
                    piece = pltpu.roll(piece, turn, 1)
                chans[ch] = jnp.where(mine, piece, chans[ch])
        for ch in range(11):
            chan_s[ch] = chans[ch]

    def place():
        for half in range(2):
            chans = [chan_s[ch, half * 8 : half * 8 + 8] for ch in range(11)]
            op_s[:, half * SZ : half * SZ + SZ] = columns(chans[:10], 0)
            goal_s[:, half * SZ : half * SZ + SZ] = chans[10]

    def layer_one(y):
        at = y * WIDE
        pre = dot(first_w[y], op_s[...])
        h_one_s[0:HID, at : at + WIDE] = jnp.tanh(pre[0:HID].astype(bf16))
        f_s[:, at : at + WIDE] = pre[HID : HID + 16].astype(bf16)

    def layer_two(y):
        at = y * WIDE
        pre = dot(mid_w[...], h_one_s[:, at : at + WIDE])
        h_two = jnp.tanh(pre.astype(bf16))
        h_two_s[:, at : at + WIDE] = h_two
        return dot(out_w[y], h_two)

    def errors(k, logit):
        live = jnp.where(
            (lane8 // 16) % 2 == 0, tab[2, k * CAP].astype(f32), tab[2, k * CAP + 1].astype(f32)
        )
        visc = eddy_scale * softplus(logit)
        delta = live * (visc - goal_s[...]) * eddy_scale * sigmoid(logit)
        row_s[...] = delta.astype(bf16).astype(f32)

    def output_side(y):
        at = y * WIDE
        d_s[:, at : at + WIDE] = jnp.broadcast_to(row_s[y : y + 1], (16, WIDE)).astype(bf16)
        for half in range(2):
            to = at + half * SZ
            row = jnp.broadcast_to(row_s[y : y + 1, half * SZ : half * SZ + SZ], (HID, SZ))
            act = h_two_s[:, to : to + SZ].astype(f32)
            d_two_s[:, to : to + SZ] = (out_wide * row * (1.0 - act * act)).astype(bf16)

    def input_side(y):
        at = y * WIDE
        back = dot(mid_t[...], d_two_s[:, at : at + WIDE])
        act = h_one_s[0:HID, at : at + WIDE].astype(f32)
        d_one_s[:, at : at + WIDE] = (back * (1.0 - act * act)).astype(bf16)

    def add_output(y):
        span = slice(y * WIDE, (y + 1) * WIDE)
        acc_mid[...] += dot_nt(h_one_s[:, span], d_two_s[:, span])
        acc_out[...] += dot_nt(d_s[:, span], h_two_s[:, span])

    def add_input(y):
        span = slice(y * WIDE, (y + 1) * WIDE)
        acc_in[...] += dot_nt(f_s[:, span], d_one_s[:, span])

    assemble(0)
    place()
    for y in range(8):
        layer_one(y)
    logit = jnp.zeros((16, WIDE), f32)
    for y in range(8):
        logit = logit + layer_two(y)
    errors(0, logit[:8])
    assemble(1)
    place()

    def tile(i, carry):
        @pl.when(i % 4 == 0)
        def _():
            acc_mid[...] = jnp.zeros(acc_mid.shape, f32)
            acc_in[...] = jnp.zeros(acc_in.shape, f32)
            acc_out[...] = jnp.zeros(acc_out.shape, f32)

        assemble(jnp.minimum(i + 2, 15))
        logit = jnp.zeros((16, WIDE), f32)
        for step in range(8 + max(LAGS)):
            at = [step - lag for lag in LAGS]
            if 0 <= at[0] < 8:
                output_side(at[0])
            if 0 <= at[1] < 8:
                input_side(at[1])
            if 0 <= at[2] < 8:
                add_output(at[2])
            if 0 <= at[3] < 8:
                add_input(at[3])
                layer_one(at[3])
            if 0 <= at[4] < 8:
                logit = logit + layer_two(at[4])
        errors(jnp.minimum(i + 1, 15) // 4, logit[:8])
        place()

        @pl.when(i % 4 == 3)
        def _():
            k = i // 4
            stage[0:HID] = acc_mid[0:HID]
            stage[HID : HID + 1] = acc_mid[HID : HID + 1]
            stage[HID + 1 : HID + 2] = acc_in[FEAT : FEAT + 1]
            stage[HID + 2 : HID + 3] = acc_out[0:1]
            stage[HID + 8 : HID + 8 + FEAT] = acc_in[0:FEAT]
            for q in range(4):
                grads[q, k] = stage[q * QROWS : (q + 1) * QROWS]

        return carry

    lax.fori_loop(0, 16, tile, 0)


def patch_grads(gy, count, corner, dest, v, halos, target, weights, mid_t, out_col):
    return pl.pallas_call(
        patch_kernel,
        out_shape=jax.ShapeDtypeStruct((4, TRAINERS, QROWS, SZ), f32),
        in_specs=smem(4) + whole(13),
        out_specs=pl.BlockSpec(memory_space=pltpu.VMEM),
        scratch_shapes=[
            pltpu.SMEM((4, 8), jnp.int32),
            pltpu.VMEM((3, SX + 2, 48, SZ), f32),
            pltpu.VMEM((9, SX, SY, SZ), f32),
            pltpu.VMEM((SY, SZ), f32),
            pltpu.VMEM((SX, SY, SZ), f32),
            pltpu.VMEM((FEAT + 1, PATCH, SZ), f32),
            pltpu.VMEM((96, WIDE), bf16),
            pltpu.VMEM((8, WIDE), f32),
            pltpu.VMEM((HID + 16, 8 * WIDE), bf16),
            pltpu.VMEM((HID, 8 * WIDE), bf16),
            pltpu.VMEM((HID, 8 * WIDE), bf16),
            pltpu.VMEM((HID, 8 * WIDE), bf16),
            pltpu.VMEM((16, 8 * WIDE), bf16),
            pltpu.VMEM((16, 8 * WIDE), bf16),
            pltpu.VMEM((8, WIDE), f32),
            pltpu.VMEM((HID + 16, SZ), f32),
            pltpu.VMEM((16, SZ), f32),
            pltpu.VMEM((16, SZ), f32),
            pltpu.VMEM((ROWS, SZ), f32),
        ],
        name="patch_grads",
    )(gy, count, corner, dest, v, *halos, target, *weights, mid_t, out_col)


def gather_kernel(parts, out):
    total = parts[0]
    for i in range(1, 16):
        total = total + parts[i]
    square = jnp.sum(total * total)
    full = jnp.concatenate([total, jnp.zeros((SZ - QROWS, SZ), f32)], 0)
    out[...] = jnp.where(lanes_of((SZ, SZ)) == QROWS, square, full.T)


def scale_kernel(parts, out):
    x = parts[...].reshape(8, 2, 8, SZ)
    folded = x[:, 0] + x[:, 1]
    folded = folded.reshape(64, SZ)
    sub = sublanes_of((64, SZ))
    swapped = jnp.where(
        sub % 8 < 4, pltpu.roll(folded, 60, 0), pltpu.roll(folded, 4, 0)
    )
    norms = (folded + swapped)[:, QROWS : QROWS + 1]
    factor = jnp.broadcast_to(grad_gain / jnp.sqrt(norms + norm_epsilon), (64, SZ))
    scaled = x * factor.reshape(8, 1, 8, SZ)
    total = scaled[0]
    for i in range(1, 8):
        total = total + scaled[i]
    lane = lanes_of((1, SZ))
    quarters = []
    for q in range(4):
        rows = total[q // 2][(q % 2) * 4 : (q % 2) * 4 + 4]
        quarters.append(jnp.where(lane < QROWS, jnp.sum(rows, axis=0, keepdims=True), 0.0))
    left = quarters[0] + pltpu.roll(quarters[1], 40, 1) + pltpu.roll(quarters[2], 80, 1)
    tail = pltpu.roll(quarters[3], 120, 1)
    left = left + jnp.where(lane >= 120, tail, 0.0)
    right = jnp.where(lane < 32, tail, 0.0)
    row = jnp.concatenate([left, right], 1)
    out[...] = jnp.broadcast_to(row.reshape(1, 1, 2 * SZ), (SZ, 1, 2 * SZ))


def final_kernel(parts, mid, rest_in, bias_in, bias_mid, rest_out):
    mid[...] = parts[:, 0, 0:SZ]
    tail = parts[:, 0, SZ : 2 * SZ].T
    bias_mid[...] = tail[0:1]
    bias_in[...] = tail[1:2]
    rest_out[...] = tail[2:3]
    rest_in[...] = tail[8 : 8 + FEAT]


def call(kernel, outs, *args):
    return pl.pallas_call(
        kernel, out_shape=outs, in_specs=whole(len(args)),
        out_specs=jax.tree.map(lambda _: pl.BlockSpec(memory_space=pltpu.VMEM), outs),
        name=kernel.__name__,
    )(*args)


def struct(*shape):
    return jax.ShapeDtypeStruct(shape, f32)


def bias_rows(bias):
    high = bias.astype(bf16).astype(f32)
    middle = (bias - high).astype(bf16).astype(f32)
    low = bias - high - middle
    sub = sublanes_of((16, HID))
    rows = jnp.where(sub == 0, high, jnp.where(sub == 1, middle, jnp.where(sub == 2, low, 0.0)))
    return rows.astype(bf16)


def one_hot(shape, test):
    return jnp.where(test(sublanes_of(shape), lanes_of(shape)), 1.0, 0.0).astype(bf16)


def prepare_kernel(w_in, b_in, w_mid, b_mid, w_out, first_w, mid_w, mid_t, out_w, out_col):
    eye = one_hot((HID, HID), lambda i, j: i == j)
    bias = dot_nt(eye, bias_rows(b_in[...])).astype(bf16)
    bias_part = dot(bias, one_hot((16, 96), lambda i, j: j == 80 + i))
    first = dot_nt(eye, w_in[...]).astype(bf16)
    row = jnp.broadcast_to(w_out[...], (16, HID))
    sub = sublanes_of((16, HID))
    for y in range(8):
        spread = one_hot((FEAT, 96), lambda i, j: j == i * 8 + y)
        first_w[y, 0:HID] = (dot(first, spread) + bias_part).astype(bf16)
        first_w[y, HID : HID + 16] = one_hot(
            (16, 96),
            lambda i, j: ((i < FEAT) & (j == i * 8 + y)) | ((i == FEAT) & (j == FEAT * 8)),
        )
        out_w[y] = jnp.where(sub == y, row.astype(f32), 0.0).astype(bf16)
    mid_w[:, 0:HID] = w_mid[...]
    mid_w[:, HID : HID + 16] = dot_nt(eye, bias_rows(b_mid[...])).astype(bf16)
    mid_t[...] = dot_nt(eye, w_mid[...]).astype(bf16)
    out_col[...] = dot_nt(eye, jnp.broadcast_to(w_out[...], (HID, HID)))


def prepare(weight_in, bias_in, weight_mid, bias_mid, weight_out):
    outs = [
        jax.ShapeDtypeStruct((8, HID + 16, 96), bf16),
        jax.ShapeDtypeStruct((HID, HID + 16), bf16),
        jax.ShapeDtypeStruct((HID, HID), bf16),
        jax.ShapeDtypeStruct((8, 16, HID), bf16),
        struct(HID, SZ),
    ]
    return call(
        prepare_kernel, outs, weight_in.T, bias_in.reshape(1, HID), weight_mid,
        bias_mid.reshape(1, HID), weight_out.reshape(1, HID),
    )


def on_device(
    velocity, target_visc, weight_in, bias_in, weight_mid, bias_mid, weight_out,
    patch_count, patch_corner, patch_dest,
):
    gy = lax.axis_index("gy").astype(jnp.int32).reshape(1)
    first_w, mid_w, mid_t, out_w, out_col = prepare(
        weight_in, bias_in, weight_mid, bias_mid, weight_out
    )
    net = (first_w, mid_w, out_col)
    halos = exchange(pack_faces(velocity))
    grads = patch_grads(
        gy, patch_count.reshape(1), patch_corner.reshape(SLOTS, 3).T, patch_dest.reshape(SLOTS),
        velocity, halos, target_visc, (first_w, mid_w, out_w), mid_t, out_col,
    )
    every = ("gx", "gy", "gz")
    summed = lax.all_to_all(
        grads.reshape(16, QROWS, SZ), ("gy", "gz"), split_axis=0, concat_axis=0, tiled=True
    )
    velocity_late, grads = lax.optimization_barrier((velocity, grads))
    first, *faces = section(gy, velocity_late, halos, net)
    summed, first = lax.optimization_barrier((summed, first))
    pieces = call(gather_kernel, struct(SZ, SZ), summed)
    pieces = lax.all_to_all(pieces, every, split_axis=0, concat_axis=0, tiled=True)
    halos = exchange(faces)
    pieces, halos = lax.optimization_barrier((pieces, halos))
    column = call(scale_kernel, struct(SZ, 1, 2 * SZ), pieces)
    table = lax.all_to_all(column, every, split_axis=0, concat_axis=0, tiled=True)
    first, column = lax.optimization_barrier((first, column))
    (new_velocity,) = section(gy, first, halos, net, velocity)
    table, new_velocity = lax.optimization_barrier((table, new_velocity))
    grad_mid, grad_in, grad_b_in, grad_b_mid, grad_out = call(
        final_kernel,
        [struct(HID, HID), struct(FEAT, HID), struct(1, HID), struct(1, HID), struct(1, HID)],
        table,
    )
    return (
        new_velocity, grad_in.T, grad_b_in.reshape(HID), grad_mid, grad_b_mid.reshape(HID),
        grad_out.reshape(HID),
    )


def solution(mesh):
    in_specs = (
        P(None, "gx", "gy", "gz"),
        P("gx", "gy", "gz"),
        P(), P(), P(), P(), P(),
        P("gx", "gy", "gz"),
        P("gx", "gy", "gz", None, None),
        P("gx", "gy", "gz", None),
    )
    out_specs = (P(None, "gx", "gy", "gz"), P(), P(), P(), P(), P())
    return jax.shard_map(
        on_device, mesh=mesh, in_specs=in_specs, out_specs=out_specs, check_vma=False
    )
```

```python
import jax
import jax.numpy as jnp
from jax import lax
from jax.experimental import pallas as pl
from jax.experimental.pallas import tpu as pltpu
from jax.sharding import PartitionSpec as P

SX, SY, SZ = 16, 32, 128
HID = 128
FEAT = 10
PATCH = 16
CAP = 2
TRAINERS = 4
SLOTS = CAP * TRAINERS
ROWS = 160
QROWS = ROWS // 4
WIDE = 2 * SZ
LAGS = (0, 1, 2, 3, 5)

time_step = 0.2
base_viscosity = 0.02
eddy_scale = 0.1
grad_gain = 20.0
norm_epsilon = 1e-06

SMALL = pltpu.CompilerParams(vmem_limit_bytes=8 << 20)
ROOMY = pltpu.CompilerParams(vmem_limit_bytes=24 << 20)

f32 = jnp.float32
bf16 = jnp.bfloat16


def lanes_of(shape):
    return lax.broadcasted_iota(jnp.int32, shape, len(shape) - 1)


def sublanes_of(shape):
    return lax.broadcasted_iota(jnp.int32, shape, len(shape) - 2)


def softplus(x):
    return jnp.maximum(x, 0.0) + jnp.log1p(jnp.exp(-jnp.abs(x)))


def sigmoid(x):
    e = jnp.exp(-jnp.abs(x))
    return jnp.where(x >= 0, 1.0, e) / (1.0 + e)


def dot(a, b):
    return lax.dot_general(a, b, (((1,), (0,)), ((), ())), preferred_element_type=f32)


def dot_nt(a, b):
    return lax.dot_general(a, b, (((1,), (1,)), ((), ())), preferred_element_type=f32)


def wall_plane(gy):
    rows = (gy * SY + sublanes_of((SY, SZ))).astype(f32)
    return 1.0 - jnp.abs(2.0 * (rows + 0.5) / (SY * 4) - 1.0)


def put_faces(x, planes, xlo, xhi, ylo, yhi, zlo, zhi):
    lane = lanes_of((SY, SZ))
    low, high = zlo[...], zhi[...]
    for c in range(3):
        plane = planes[c]
        ylo[c, pl.ds(x, 1), :] = plane[0:1]
        yhi[c, pl.ds(x, 1), :] = plane[SY - 1 : SY]
        here = lane == c * SX + x
        low = jnp.where(here, jnp.broadcast_to(plane[:, 0:1], (SY, SZ)), low)
        high = jnp.where(here, jnp.broadcast_to(plane[:, SZ - 1 : SZ], (SY, SZ)), high)
    zlo[...] = low
    zhi[...] = high


def faces_kernel(v, xlo, xhi, ylo, yhi, zlo, zhi):
    zlo[...] = jnp.zeros((SY, SZ), f32)
    zhi[...] = jnp.zeros((SY, SZ), f32)
    xlo[...] = v[:, 0]
    xhi[...] = v[:, SX - 1]

    def step(i, carry):
        for x in [i * 4 + j for j in range(4)]:
            put_faces(x, [v[c, x] for c in range(3)], xlo, xhi, ylo, yhi, zlo, zhi)
        return carry

    lax.fori_loop(0, SX // 4, step, 0)


FACE_SHAPES = ((3, SY, SZ),) * 2 + ((3, SX, SZ),) * 2 + ((SY, SZ),) * 2


def face_structs():
    return [jax.ShapeDtypeStruct(s, f32) for s in FACE_SHAPES]


def whole(n):
    return [pl.BlockSpec(memory_space=pltpu.VMEM) for _ in range(n)]


def smem(n):
    return [pl.BlockSpec(memory_space=pltpu.SMEM) for _ in range(n)]


def pack_faces(v):
    return pl.pallas_call(
        faces_kernel, out_shape=face_structs(), in_specs=whole(1), out_specs=whole(6), name="faces",
        compiler_params=SMALL,
    )(v)


def exchange(faces):
    xlo, xhi, ylo, yhi, zlo, zhi = faces

    def shift(low, high, axis, closed):
        count = lax.axis_size(axis)
        ends = count if closed else count - 1
        from_low = lax.ppermute(high, axis, [(i, (i + 1) % count) for i in range(ends)])
        from_high = lax.ppermute(low, axis, [((i + 1) % count, i) for i in range(ends)])
        return from_low, from_high

    return (
        shift(xlo, xhi, "gx", True) + shift(ylo, yhi, "gy", False) + shift(zlo, zhi, "gz", True)
    )


def fill_padded(v, halos, pad):
    hx0, hx1, hy0, hy1 = halos[:4]
    for c in range(3):
        pad[c, 0, 8 : 8 + SY] = hx0[c]
        pad[c, SX + 1, 8 : 8 + SY] = hx1[c]

    def step(i, carry):
        for x in [i * 4 + j for j in range(4)]:
            for c in range(3):
                pad[c, x + 1, 8 : 8 + SY] = v[c, x]
                pad[c, x + 1, 7:8] = hy0[c, pl.ds(x, 1), :]
                pad[c, x + 1, 8 + SY : 9 + SY] = hy1[c, pl.ds(x, 1), :]
        return carry

    lax.fori_loop(0, SX // 4, step, 0)


def stencil(x, pad, hz0, hz1):
    lane = lanes_of((SY, SZ))
    low, high = hz0[...], hz1[...]
    centers, dxs, dys, dzs, laps = [], [], [], [], []
    for c in range(3):
        at = c * SX + x
        ctr = pad[c, x + 1, 8 : 8 + SY]
        xm, xp = pad[c, x, 8 : 8 + SY], pad[c, x + 2, 8 : 8 + SY]
        ym, yp = pad[c, x + 1, 7 : 7 + SY], pad[c, x + 1, 9 : 9 + SY]
        zm = jnp.where(lane == 0, pltpu.roll(low, (SZ - at) % SZ, 1), pltpu.roll(ctr, 1, 1))
        zp = jnp.where(
            lane == SZ - 1, pltpu.roll(high, SZ - 1 - at, 1), pltpu.roll(ctr, SZ - 1, 1)
        )
        centers.append(ctr)
        dxs.append((xp - xm) * 0.5)
        dys.append((yp - ym) * 0.5)
        dzs.append((zp - zm) * 0.5)
        laps.append(xp + xm + yp + ym + zp + zm - 6.0 * ctr)
    return centers, dxs, dys, dzs, laps


def columns(channels, group):
    parts = [ch[group * 8 : group * 8 + 8] for ch in channels]
    parts.append(jnp.ones((16, SZ), f32))
    return jnp.concatenate(parts, 0).astype(bf16)


def section_kernel(second, *refs):
    gy = refs[0]
    v, *halos = refs[1:8]
    at = 8
    if second:
        velocity = refs[at]
        at += 1
    first_w, mid_w, out_col = refs[at : at + 3]
    at += 3
    new = refs[at]
    at += 1
    if not second:
        faces = refs[at : at + 6]
        at += 6
    pad, op_s, h_one_s, logit_s, adv_s, lap_s = refs[at : at + 6]
    fill_padded(v, halos, pad)
    wall = wall_plane(gy[0])
    h_one_s[HID : HID + 16] = jnp.ones((16, 16 * WIDE), bf16)
    if not second:
        faces[4][...] = jnp.zeros((SY, SZ), f32)
        faces[5][...] = jnp.zeros((SY, SZ), f32)

    def begin(x):
        centers, dxs, dys, dzs, laps = stencil(x, pad, halos[4], halos[5])
        chans = dxs + dys + dzs + [wall]
        for group in range(4):
            op_s[:, group * SZ : group * SZ + SZ] = columns(chans, group)
        slot = x % 4
        for c in range(3):
            adv_s[slot, c] = centers[0] * dxs[c] + centers[1] * dys[c] + centers[2] * dzs[c]
            lap_s[slot, c] = laps[c]

    def finish(x, slot):
        visc = base_viscosity + eddy_scale * softplus(logit_s[...])
        planes = []
        for c in range(3):
            rate = visc * lap_s[slot, c] - adv_s[slot, c]
            moved = pad[c, x + 1, 8 : 8 + SY] + time_step * rate
            if second:
                moved = 0.5 * velocity[c, x] + 0.5 * moved
            new[c, x] = moved
            planes.append(moved)
        if not second:
            put_faces(x, planes, *faces)

    def layer_one(i):
        operand = op_s[:, i // 8 * WIDE : i // 8 * WIDE + WIDE]
        pre = dot(first_w[i % 8, 0:HID], operand)
        h_one_s[0:HID, i * WIDE : i * WIDE + WIDE] = jnp.tanh(pre.astype(bf16))

    def layer_two(i):
        pre = dot(mid_w[...], h_one_s[:, i * WIDE : i * WIDE + WIDE])
        h_two = jnp.tanh(pre.astype(bf16)).astype(f32)
        for half in range(2):
            to = ((i // 8) * 2 + half) * 8 + i % 8
            terms = h_two[:, half * SZ : half * SZ + SZ] * out_col[...]
            logit_s[to : to + 1] = jnp.sum(terms, axis=0, keepdims=True)

    begin(0)
    for i in range(16):
        layer_one(i)
    begin(1)

    def step(x, carry):
        finish(jnp.maximum(x - 1, 0), (x + 3) % 4)
        for i in range(16):
            layer_two(i)
            layer_one(i)
        begin(jnp.minimum(x + 2, SX - 1))
        return carry

    lax.fori_loop(0, SX, step, 0)
    finish(SX - 1, (SX - 1) % 4)
    if not second:
        faces[0][...] = new[:, 0]
        faces[1][...] = new[:, SX - 1]


def section(gy, v, halos, weights, velocity=None):
    second = velocity is not None
    outs = [jax.ShapeDtypeStruct((3, SX, SY, SZ), f32)]
    if not second:
        outs += face_structs()
    args = [gy, v, *halos] + ([velocity] if second else []) + list(weights)
    return pl.pallas_call(
        lambda *refs: section_kernel(second, *refs),
        out_shape=outs,
        in_specs=smem(1) + whole(len(args) - 1),
        out_specs=whole(len(outs)),
        scratch_shapes=[
            pltpu.VMEM((3, SX + 2, 48, SZ), f32),
            pltpu.VMEM((96, 4 * SZ), bf16),
            pltpu.VMEM((HID + 16, 16 * WIDE), bf16),
            pltpu.VMEM((SY, SZ), f32),
            pltpu.VMEM((4, 3, SY, SZ), f32),
            pltpu.VMEM((4, 3, SY, SZ), f32),
        ],
        compiler_params=ROOMY,
        name="section_two" if second else "section_one",
    )(*args)


def patch_kernel(
    gy, count, corner, dest, v, hx0, hx1, hy0, hy1, hz0, hz1, target,
    first_w, mid_w, out_w, mid_t, out_col, grads,
    tab, pad, feats, wall_s, tgt_s, chan_s, op_s, goal_s, h_one_s, h_two_s, d_one_s, d_two_s, f_s, d_s, row_s,
    acc_mid, acc_in, acc_out, stage,
):
    for t in range(TRAINERS):
        tab[3, t] = 0
    for s in range(SLOTS):
        d = dest[s]
        rank = tab[3, d]
        tab[3, d] = rank + 1
        spot = d * CAP + rank
        tab[0, spot] = corner[1, s]
        tab[1, spot] = corner[2, s]
        tab[2, spot] = jnp.where(s < count[0], 1, 0)
    wall_s[...] = wall_plane(gy[0])
    fill_padded(v, (hx0, hx1, hy0, hy1), pad)

    def plane(i, carry):
        for x in [i * 2, i * 2 + 1]:
            _, dxs, dys, dzs, _ = stencil(x, pad, hz0, hz1)
            for f, diff in enumerate(dxs + dys + dzs):
                feats[f, x] = diff
            tgt_s[x] = target[x].astype(f32)
        return carry

    lax.fori_loop(0, SX // 2, plane, 0)
    h_one_s[HID : HID + 16] = jnp.ones((16, 8 * WIDE), bf16)
    stage[...] = jnp.zeros((ROWS, SZ), f32)
    lane = lanes_of((PATCH, SZ))
    lane8 = lanes_of((8, WIDE))
    out_wide = out_col[...]

    def assemble(i):
        k = i // 4
        xo = i % 4
        chans = [jnp.zeros((PATCH, SZ), f32) for _ in range(11)]
        for q in range(8):
            xi, r = q // 2, q % 2
            spot = k * CAP + r
            cy, cz = tab[0, spot], tab[1, spot]
            x = xo * 4 + xi
            mine = lane // 16 == q
            turn = lax.rem(q * 16 - cz + SZ, SZ)
            for ch in range(11):
                if ch == 9:
                    piece = wall_s[pl.ds(cy, PATCH), :]
                elif ch == 10:
                    piece = tgt_s[x, pl.ds(cy, PATCH), :]
                else:
                    piece = feats[ch, x, pl.ds(cy, PATCH), :]
                if ch != 9:
                    piece = pltpu.roll(piece, turn, 1)
                chans[ch] = jnp.where(mine, piece, chans[ch])
        for ch in range(11):
            chan_s[ch] = chans[ch]

    def place():
        for half in range(2):
            chans = [chan_s[ch, half * 8 : half * 8 + 8] for ch in range(11)]
            op_s[:, half * SZ : half * SZ + SZ] = columns(chans[:10], 0)
            goal_s[:, half * SZ : half * SZ + SZ] = chans[10]

    def layer_one(y):
        at = y * WIDE
        pre = dot(first_w[y], op_s[...])
        h_one_s[0:HID, at : at + WIDE] = jnp.tanh(pre[0:HID].astype(bf16))
        f_s[:, at : at + WIDE] = pre[HID : HID + 16].astype(bf16)

    def layer_two(y):
        at = y * WIDE
        pre = dot(mid_w[...], h_one_s[:, at : at + WIDE])
        h_two = jnp.tanh(pre.astype(bf16))
        h_two_s[:, at : at + WIDE] = h_two
        return dot(out_w[y], h_two)

    def errors(k, logit):
        live = jnp.where(
            (lane8 // 16) % 2 == 0, tab[2, k * CAP].astype(f32), tab[2, k * CAP + 1].astype(f32)
        )
        visc = eddy_scale * softplus(logit)
        delta = live * (visc - goal_s[...]) * eddy_scale * sigmoid(logit)
        row_s[...] = delta.astype(bf16).astype(f32)

    def output_side(y):
        at = y * WIDE
        d_s[:, at : at + WIDE] = jnp.broadcast_to(row_s[y : y + 1], (16, WIDE)).astype(bf16)
        for half in range(2):
            to = at + half * SZ
            row = jnp.broadcast_to(row_s[y : y + 1, half * SZ : half * SZ + SZ], (HID, SZ))
            act = h_two_s[:, to : to + SZ].astype(f32)
            d_two_s[:, to : to + SZ] = (out_wide * row * (1.0 - act * act)).astype(bf16)

    def input_side(y):
        at = y * WIDE
        back = dot(mid_t[...], d_two_s[:, at : at + WIDE])
        act = h_one_s[0:HID, at : at + WIDE].astype(f32)
        d_one_s[:, at : at + WIDE] = (back * (1.0 - act * act)).astype(bf16)

    def add_output(y):
        span = slice(y * WIDE, (y + 1) * WIDE)
        acc_mid[...] += dot_nt(h_one_s[:, span], d_two_s[:, span])
        acc_out[...] += dot_nt(d_s[:, span], h_two_s[:, span])

    def add_input(y):
        span = slice(y * WIDE, (y + 1) * WIDE)
        acc_in[...] += dot_nt(f_s[:, span], d_one_s[:, span])

    assemble(0)
    place()
    for y in range(8):
        layer_one(y)
    logit = jnp.zeros((16, WIDE), f32)
    for y in range(8):
        logit = logit + layer_two(y)
    errors(0, logit[:8])
    assemble(1)
    place()

    def tile(i, carry):
        @pl.when(i % 4 == 0)
        def _():
            acc_mid[...] = jnp.zeros(acc_mid.shape, f32)
            acc_in[...] = jnp.zeros(acc_in.shape, f32)
            acc_out[...] = jnp.zeros(acc_out.shape, f32)

        assemble(jnp.minimum(i + 2, 15))
        logit = jnp.zeros((16, WIDE), f32)
        for step in range(8 + max(LAGS)):
            at = [step - lag for lag in LAGS]
            if 0 <= at[0] < 8:
                output_side(at[0])
            if 0 <= at[1] < 8:
                input_side(at[1])
            if 0 <= at[2] < 8:
                add_output(at[2])
            if 0 <= at[3] < 8:
                add_input(at[3])
                layer_one(at[3])
            if 0 <= at[4] < 8:
                logit = logit + layer_two(at[4])
        errors(jnp.minimum(i + 1, 15) // 4, logit[:8])
        place()

        @pl.when(i % 4 == 3)
        def _():
            k = i // 4
            stage[0:HID] = acc_mid[0:HID]
            stage[HID : HID + 1] = acc_mid[HID : HID + 1]
            stage[HID + 1 : HID + 2] = acc_in[FEAT : FEAT + 1]
            stage[HID + 2 : HID + 3] = acc_out[0:1]
            stage[HID + 8 : HID + 8 + FEAT] = acc_in[0:FEAT]
            for q in range(4):
                grads[q, k] = stage[q * QROWS : (q + 1) * QROWS]

        return carry

    lax.fori_loop(0, 16, tile, 0)


def patch_grads(gy, count, corner, dest, v, halos, target, weights, mid_t, out_col):
    return pl.pallas_call(
        patch_kernel,
        out_shape=jax.ShapeDtypeStruct((4, TRAINERS, QROWS, SZ), f32),
        in_specs=smem(4) + whole(13),
        out_specs=pl.BlockSpec(memory_space=pltpu.VMEM),
        scratch_shapes=[
            pltpu.SMEM((4, 8), jnp.int32),
            pltpu.VMEM((3, SX + 2, 48, SZ), f32),
            pltpu.VMEM((9, SX, SY, SZ), f32),
            pltpu.VMEM((SY, SZ), f32),
            pltpu.VMEM((SX, SY, SZ), f32),
            pltpu.VMEM((FEAT + 1, PATCH, SZ), f32),
            pltpu.VMEM((96, WIDE), bf16),
            pltpu.VMEM((8, WIDE), f32),
            pltpu.VMEM((HID + 16, 8 * WIDE), bf16),
            pltpu.VMEM((HID, 8 * WIDE), bf16),
            pltpu.VMEM((HID, 8 * WIDE), bf16),
            pltpu.VMEM((HID, 8 * WIDE), bf16),
            pltpu.VMEM((16, 8 * WIDE), bf16),
            pltpu.VMEM((16, 8 * WIDE), bf16),
            pltpu.VMEM((8, WIDE), f32),
            pltpu.VMEM((HID + 16, SZ), f32),
            pltpu.VMEM((16, SZ), f32),
            pltpu.VMEM((16, SZ), f32),
            pltpu.VMEM((ROWS, SZ), f32),
        ],
        compiler_params=pltpu.CompilerParams(
            vmem_limit_bytes=28 << 20
        ),
        name="patch_grads",
    )(gy, count, corner, dest, v, *halos, target, *weights, mid_t, out_col)


def gather_kernel(parts, out):
    total = parts[0]
    for i in range(1, 16):
        total = total + parts[i]
    square = jnp.sum(total * total)
    full = jnp.concatenate([total, jnp.zeros((SZ - QROWS, SZ), f32)], 0)
    out[...] = jnp.where(lanes_of((SZ, SZ)) == QROWS, square, full.T)


def scale_kernel(parts, out):
    x = parts[...].reshape(8, 2, 8, SZ)
    folded = x[:, 0] + x[:, 1]
    folded = folded.reshape(64, SZ)
    sub = sublanes_of((64, SZ))
    swapped = jnp.where(
        sub % 8 < 4, pltpu.roll(folded, 60, 0), pltpu.roll(folded, 4, 0)
    )
    norms = (folded + swapped)[:, QROWS : QROWS + 1]
    factor = jnp.broadcast_to(grad_gain / jnp.sqrt(norms + norm_epsilon), (64, SZ))
    scaled = x * factor.reshape(8, 1, 8, SZ)
    total = scaled[0]
    for i in range(1, 8):
        total = total + scaled[i]
    lane = lanes_of((1, SZ))
    quarters = []
    for q in range(4):
        rows = total[q // 2][(q % 2) * 4 : (q % 2) * 4 + 4]
        quarters.append(jnp.where(lane < QROWS, jnp.sum(rows, axis=0, keepdims=True), 0.0))
    left = quarters[0] + pltpu.roll(quarters[1], 40, 1) + pltpu.roll(quarters[2], 80, 1)
    tail = pltpu.roll(quarters[3], 120, 1)
    left = left + jnp.where(lane >= 120, tail, 0.0)
    right = jnp.where(lane < 32, tail, 0.0)
    row = jnp.concatenate([left, right], 1)
    out[...] = jnp.broadcast_to(row.reshape(1, 1, 2 * SZ), (SZ, 1, 2 * SZ))


def final_kernel(parts, mid, rest_in, bias_in, bias_mid, rest_out):
    mid[...] = parts[:, 0, 0:SZ]
    tail = parts[:, 0, SZ : 2 * SZ].T
    bias_mid[...] = tail[0:1]
    bias_in[...] = tail[1:2]
    rest_out[...] = tail[2:3]
    rest_in[...] = tail[8 : 8 + FEAT]


def call(kernel, outs, *args):
    return pl.pallas_call(
        kernel, out_shape=outs, in_specs=whole(len(args)),
        out_specs=jax.tree.map(lambda _: pl.BlockSpec(memory_space=pltpu.VMEM), outs),
        compiler_params=SMALL, name=kernel.__name__,
    )(*args)


def struct(*shape):
    return jax.ShapeDtypeStruct(shape, f32)


def bias_rows(bias):
    high = bias.astype(bf16).astype(f32)
    middle = (bias - high).astype(bf16).astype(f32)
    low = bias - high - middle
    sub = sublanes_of((16, HID))
    rows = jnp.where(sub == 0, high, jnp.where(sub == 1, middle, jnp.where(sub == 2, low, 0.0)))
    return rows.astype(bf16)


def one_hot(shape, test):
    return jnp.where(test(sublanes_of(shape), lanes_of(shape)), 1.0, 0.0).astype(bf16)


def prepare_kernel(w_in, b_in, w_mid, b_mid, w_out, first_w, mid_w, mid_t, out_w, out_col):
    eye = one_hot((HID, HID), lambda i, j: i == j)
    bias = dot_nt(eye, bias_rows(b_in[...])).astype(bf16)
    bias_part = dot(bias, one_hot((16, 96), lambda i, j: j == 80 + i))
    first = dot_nt(eye, w_in[...]).astype(bf16)
    row = jnp.broadcast_to(w_out[...], (16, HID))
    sub = sublanes_of((16, HID))
    for y in range(8):
        spread = one_hot((FEAT, 96), lambda i, j: j == i * 8 + y)
        first_w[y, 0:HID] = (dot(first, spread) + bias_part).astype(bf16)
        first_w[y, HID : HID + 16] = one_hot(
            (16, 96),
            lambda i, j: ((i < FEAT) & (j == i * 8 + y)) | ((i == FEAT) & (j == FEAT * 8)),
        )
        out_w[y] = jnp.where(sub == y, row.astype(f32), 0.0).astype(bf16)
    mid_w[:, 0:HID] = w_mid[...]
    mid_w[:, HID : HID + 16] = dot_nt(eye, bias_rows(b_mid[...])).astype(bf16)
    mid_t[...] = dot_nt(eye, w_mid[...]).astype(bf16)
    out_col[...] = dot_nt(eye, jnp.broadcast_to(w_out[...], (HID, HID)))


def prepare(weight_in, bias_in, weight_mid, bias_mid, weight_out):
    outs = [
        jax.ShapeDtypeStruct((8, HID + 16, 96), bf16),
        jax.ShapeDtypeStruct((HID, HID + 16), bf16),
        jax.ShapeDtypeStruct((HID, HID), bf16),
        jax.ShapeDtypeStruct((8, 16, HID), bf16),
        struct(HID, SZ),
    ]
    return call(
        prepare_kernel, outs, weight_in.T, bias_in.reshape(1, HID), weight_mid,
        bias_mid.reshape(1, HID), weight_out.reshape(1, HID),
    )


def on_device(
    velocity, target_visc, weight_in, bias_in, weight_mid, bias_mid, weight_out,
    patch_count, patch_corner, patch_dest,
):
    gy = lax.axis_index("gy").astype(jnp.int32).reshape(1)
    first_w, mid_w, mid_t, out_w, out_col = prepare(
        weight_in, bias_in, weight_mid, bias_mid, weight_out
    )
    net = (first_w, mid_w, out_col)
    halos = exchange(pack_faces(velocity))
    grads = patch_grads(
        gy, patch_count.reshape(1), patch_corner.reshape(SLOTS, 3).T, patch_dest.reshape(SLOTS),
        velocity, halos, target_visc, (first_w, mid_w, out_w), mid_t, out_col,
    )
    every = ("gx", "gy", "gz")
    summed = lax.all_to_all(
        grads.reshape(16, QROWS, SZ), ("gy", "gz"), split_axis=0, concat_axis=0, tiled=True
    )
    velocity_late, grads = lax.optimization_barrier((velocity, grads))
    first, *faces = section(gy, velocity_late, halos, net)
    summed, first = lax.optimization_barrier((summed, first))
    pieces = call(gather_kernel, struct(SZ, SZ), summed)
    pieces = lax.all_to_all(pieces, every, split_axis=0, concat_axis=0, tiled=True)
    halos = exchange(faces)
    pieces, halos = lax.optimization_barrier((pieces, halos))
    column = call(scale_kernel, struct(SZ, 1, 2 * SZ), pieces)
    table = lax.all_to_all(column, every, split_axis=0, concat_axis=0, tiled=True)
    first, column = lax.optimization_barrier((first, column))
    (new_velocity,) = section(gy, first, halos, net, velocity)
    table, new_velocity = lax.optimization_barrier((table, new_velocity))
    grad_mid, grad_in, grad_b_in, grad_b_mid, grad_out = call(
        final_kernel,
        [struct(HID, HID), struct(FEAT, HID), struct(1, HID), struct(1, HID), struct(1, HID)],
        table,
    )
    return (
        new_velocity, grad_in.T, grad_b_in.reshape(HID), grad_mid, grad_b_mid.reshape(HID),
        grad_out.reshape(HID),
    )


def solution(mesh):
    in_specs = (
        P(None, "gx", "gy", "gz"),
        P("gx", "gy", "gz"),
        P(), P(), P(), P(), P(),
        P("gx", "gy", "gz"),
        P("gx", "gy", "gz", None, None),
        P("gx", "gy", "gz", None),
    )
    out_specs = (P(None, "gx", "gy", "gz"), P(), P(), P(), P(), P())
    return jax.shard_map(
        on_device, mesh=mesh, in_specs=in_specs, out_specs=out_specs, check_vma=False
    )
```

```python
import jax
import jax.numpy as jnp
from jax import lax
from jax.experimental import pallas as pl
from jax.experimental.pallas import tpu as pltpu
from jax.sharding import PartitionSpec as P

SX, SY, SZ = 16, 32, 128
HID = 128
FEAT = 10
PATCH = 16
CAP = 2
TRAINERS = 4
SLOTS = CAP * TRAINERS
ROWS = 160
QROWS = ROWS // 4
WIDE = 2 * SZ
LAGS = (0, 1, 2, 3, 5)

time_step = 0.2
base_viscosity = 0.02
eddy_scale = 0.1
grad_gain = 20.0
norm_epsilon = 1e-06

SMALL = pltpu.CompilerParams(vmem_limit_bytes=8 << 20)
ROOMY = pltpu.CompilerParams(vmem_limit_bytes=24 << 20)

f32 = jnp.float32
bf16 = jnp.bfloat16


def lanes_of(shape):
    return lax.broadcasted_iota(jnp.int32, shape, len(shape) - 1)


def sublanes_of(shape):
    return lax.broadcasted_iota(jnp.int32, shape, len(shape) - 2)


def softplus(x):
    return jnp.maximum(x, 0.0) + jnp.log1p(jnp.exp(-jnp.abs(x)))


def sigmoid(x):
    e = jnp.exp(-jnp.abs(x))
    return jnp.where(x >= 0, 1.0, e) / (1.0 + e)


def dot(a, b):
    return lax.dot_general(a, b, (((1,), (0,)), ((), ())), preferred_element_type=f32)


def dot_nt(a, b):
    return lax.dot_general(a, b, (((1,), (1,)), ((), ())), preferred_element_type=f32)


def wall_plane(gy):
    rows = (gy * SY + sublanes_of((SY, SZ))).astype(f32)
    return 1.0 - jnp.abs(2.0 * (rows + 0.5) / (SY * 4) - 1.0)


def put_faces(x, planes, xlo, xhi, ylo, yhi, zlo, zhi):
    lane = lanes_of((SY, SZ))
    low, high = zlo[...], zhi[...]
    for c in range(3):
        plane = planes[c]
        ylo[c, pl.ds(x, 1), :] = plane[0:1]
        yhi[c, pl.ds(x, 1), :] = plane[SY - 1 : SY]
        here = lane == c * SX + x
        low = jnp.where(here, jnp.broadcast_to(plane[:, 0:1], (SY, SZ)), low)
        high = jnp.where(here, jnp.broadcast_to(plane[:, SZ - 1 : SZ], (SY, SZ)), high)
    zlo[...] = low
    zhi[...] = high


def faces_kernel(v, xlo, xhi, ylo, yhi, zlo, zhi):
    zlo[...] = jnp.zeros((SY, SZ), f32)
    zhi[...] = jnp.zeros((SY, SZ), f32)
    xlo[...] = v[:, 0]
    xhi[...] = v[:, SX - 1]

    def step(i, carry):
        for x in [i * 4 + j for j in range(4)]:
            put_faces(x, [v[c, x] for c in range(3)], xlo, xhi, ylo, yhi, zlo, zhi)
        return carry

    lax.fori_loop(0, SX // 4, step, 0)


FACE_SHAPES = ((3, SY, SZ),) * 2 + ((3, SX, SZ),) * 2 + ((SY, SZ),) * 2


def face_structs():
    return [jax.ShapeDtypeStruct(s, f32) for s in FACE_SHAPES]


def whole(n):
    return [pl.BlockSpec(memory_space=pltpu.VMEM) for _ in range(n)]


def smem(n):
    return [pl.BlockSpec(memory_space=pltpu.SMEM) for _ in range(n)]


def pack_faces(v):
    return pl.pallas_call(
        faces_kernel, out_shape=face_structs(), in_specs=whole(1), out_specs=whole(6), name="faces",
        compiler_params=SMALL,
    )(v)


def exchange(faces):
    xlo, xhi, ylo, yhi, zlo, zhi = faces

    def shift(low, high, axis, closed):
        count = lax.axis_size(axis)
        ends = count if closed else count - 1
        from_low = lax.ppermute(high, axis, [(i, (i + 1) % count) for i in range(ends)])
        from_high = lax.ppermute(low, axis, [((i + 1) % count, i) for i in range(ends)])
        return from_low, from_high

    return (
        shift(xlo, xhi, "gx", True) + shift(ylo, yhi, "gy", False) + shift(zlo, zhi, "gz", True)
    )


def fill_padded(v, halos, pad):
    hx0, hx1, hy0, hy1 = halos[:4]
    for c in range(3):
        pad[c, 0, 8 : 8 + SY] = hx0[c]
        pad[c, SX + 1, 8 : 8 + SY] = hx1[c]

    def step(i, carry):
        for x in [i * 4 + j for j in range(4)]:
            for c in range(3):
                pad[c, x + 1, 8 : 8 + SY] = v[c, x]
                pad[c, x + 1, 7:8] = hy0[c, pl.ds(x, 1), :]
                pad[c, x + 1, 8 + SY : 9 + SY] = hy1[c, pl.ds(x, 1), :]
        return carry

    lax.fori_loop(0, SX // 4, step, 0)


def stencil(x, pad, hz0, hz1):
    lane = lanes_of((SY, SZ))
    low, high = hz0[...], hz1[...]
    centers, dxs, dys, dzs, laps = [], [], [], [], []
    for c in range(3):
        at = c * SX + x
        ctr = pad[c, x + 1, 8 : 8 + SY]
        xm, xp = pad[c, x, 8 : 8 + SY], pad[c, x + 2, 8 : 8 + SY]
        ym, yp = pad[c, x + 1, 7 : 7 + SY], pad[c, x + 1, 9 : 9 + SY]
        zm = jnp.where(lane == 0, pltpu.roll(low, (SZ - at) % SZ, 1), pltpu.roll(ctr, 1, 1))
        zp = jnp.where(
            lane == SZ - 1, pltpu.roll(high, SZ - 1 - at, 1), pltpu.roll(ctr, SZ - 1, 1)
        )
        centers.append(ctr)
        dxs.append((xp - xm) * 0.5)
        dys.append((yp - ym) * 0.5)
        dzs.append((zp - zm) * 0.5)
        laps.append(xp + xm + yp + ym + zp + zm - 6.0 * ctr)
    return centers, dxs, dys, dzs, laps


def columns(channels, group):
    parts = [ch[group * 8 : group * 8 + 8] for ch in channels]
    parts.append(jnp.ones((16, SZ), f32))
    return jnp.concatenate(parts, 0).astype(bf16)


def section_kernel(second, *refs):
    gy = refs[0]
    v, *halos = refs[1:8]
    at = 8
    if second:
        velocity = refs[at]
        at += 1
    first_w, mid_w, out_col = refs[at : at + 3]
    at += 3
    new = refs[at]
    at += 1
    if not second:
        faces = refs[at : at + 6]
        at += 6
    pad, op_s, h_one_s, logit_s, adv_s, lap_s = refs[at : at + 6]
    fill_padded(v, halos, pad)
    wall = wall_plane(gy[0])
    h_one_s[HID : HID + 16] = jnp.ones((16, 16 * WIDE), bf16)
    if not second:
        faces[4][...] = jnp.zeros((SY, SZ), f32)
        faces[5][...] = jnp.zeros((SY, SZ), f32)

    def begin(x):
        centers, dxs, dys, dzs, laps = stencil(x, pad, halos[4], halos[5])
        chans = dxs + dys + dzs + [wall]
        for group in range(4):
            op_s[:, group * SZ : group * SZ + SZ] = columns(chans, group)
        slot = x % 4
        for c in range(3):
            adv_s[slot, c] = centers[0] * dxs[c] + centers[1] * dys[c] + centers[2] * dzs[c]
            lap_s[slot, c] = laps[c]

    def finish(x, slot):
        visc = base_viscosity + eddy_scale * softplus(logit_s[...])
        planes = []
        for c in range(3):
            rate = visc * lap_s[slot, c] - adv_s[slot, c]
            moved = pad[c, x + 1, 8 : 8 + SY] + time_step * rate
            if second:
                moved = 0.5 * velocity[c, x] + 0.5 * moved
            new[c, x] = moved
            planes.append(moved)
        if not second:
            put_faces(x, planes, *faces)

    def layer_one(i):
        operand = op_s[:, i // 8 * WIDE : i // 8 * WIDE + WIDE]
        pre = dot(first_w[i % 8, 0:HID], operand)
        h_one_s[0:HID, i * WIDE : i * WIDE + WIDE] = jnp.tanh(pre.astype(bf16))

    def layer_two(i):
        pre = dot(mid_w[...], h_one_s[:, i * WIDE : i * WIDE + WIDE])
        h_two = jnp.tanh(pre.astype(bf16)).astype(f32)
        for half in range(2):
            to = ((i // 8) * 2 + half) * 8 + i % 8
            terms = h_two[:, half * SZ : half * SZ + SZ] * out_col[...]
            logit_s[to : to + 1] = jnp.sum(terms, axis=0, keepdims=True)

    begin(0)
    for i in range(16):
        layer_one(i)
    begin(1)

    def step(x, carry):
        finish(jnp.maximum(x - 1, 0), (x + 3) % 4)
        for i in range(16):
            layer_two(i)
            layer_one(i)
        begin(jnp.minimum(x + 2, SX - 1))
        return carry

    lax.fori_loop(0, SX - 1, step, 0)
    finish(SX - 2, (SX - 2) % 4)
    for i in range(16):
        layer_two(i)
    finish(SX - 1, (SX - 1) % 4)
    if not second:
        faces[0][...] = new[:, 0]
        faces[1][...] = new[:, SX - 1]


def section(gy, v, halos, weights, velocity=None):
    second = velocity is not None
    outs = [jax.ShapeDtypeStruct((3, SX, SY, SZ), f32)]
    if not second:
        outs += face_structs()
    args = [gy, v, *halos] + ([velocity] if second else []) + list(weights)
    return pl.pallas_call(
        lambda *refs: section_kernel(second, *refs),
        out_shape=outs,
        in_specs=smem(1) + whole(len(args) - 1),
        out_specs=whole(len(outs)),
        scratch_shapes=[
            pltpu.VMEM((3, SX + 2, 48, SZ), f32),
            pltpu.VMEM((96, 4 * SZ), bf16),
            pltpu.VMEM((HID + 16, 16 * WIDE), bf16),
            pltpu.VMEM((SY, SZ), f32),
            pltpu.VMEM((4, 3, SY, SZ), f32),
            pltpu.VMEM((4, 3, SY, SZ), f32),
        ],
        compiler_params=ROOMY,
        name="section_two" if second else "section_one",
    )(*args)


def patch_kernel(
    gy, count, corner, dest, v, hx0, hx1, hy0, hy1, hz0, hz1, target,
    first_w, mid_w, out_w, mid_t, out_col, grads,
    tab, pad, feats, wall_s, tgt_s, chan_s, op_s, goal_s, h_one_s, h_two_s, d_one_s, d_two_s, f_s, d_s, row_s,
    acc_mid, acc_in, acc_out, stage,
):
    for t in range(TRAINERS):
        tab[3, t] = 0
    for s in range(SLOTS):
        d = dest[s]
        rank = tab[3, d]
        tab[3, d] = rank + 1
        spot = d * CAP + rank
        tab[0, spot] = corner[1, s]
        tab[1, spot] = corner[2, s]
        tab[2, spot] = jnp.where(s < count[0], 1, 0)
    wall_s[...] = wall_plane(gy[0])
    fill_padded(v, (hx0, hx1, hy0, hy1), pad)

    def plane(i, carry):
        for x in [i * 2, i * 2 + 1]:
            _, dxs, dys, dzs, _ = stencil(x, pad, hz0, hz1)
            for f, diff in enumerate(dxs + dys + dzs):
                feats[f, x] = diff
            tgt_s[x] = target[x].astype(f32)
        return carry

    lax.fori_loop(0, SX // 2, plane, 0)
    h_one_s[HID : HID + 16] = jnp.ones((16, 8 * WIDE), bf16)
    stage[...] = jnp.zeros((ROWS, SZ), f32)
    lane = lanes_of((PATCH, SZ))
    lane8 = lanes_of((8, WIDE))
    out_wide = out_col[...]

    def assemble(i):
        k = i // 4
        xo = i % 4
        chans = [jnp.zeros((PATCH, SZ), f32) for _ in range(11)]
        for q in range(8):
            xi, r = q // 2, q % 2
            spot = k * CAP + r
            cy, cz = tab[0, spot], tab[1, spot]
            x = xo * 4 + xi
            mine = lane // 16 == q
            turn = lax.rem(q * 16 - cz + SZ, SZ)
            for ch in range(11):
                if ch == 9:
                    piece = wall_s[pl.ds(cy, PATCH), :]
                elif ch == 10:
                    piece = tgt_s[x, pl.ds(cy, PATCH), :]
                else:
                    piece = feats[ch, x, pl.ds(cy, PATCH), :]
                if ch != 9:
                    piece = pltpu.roll(piece, turn, 1)
                chans[ch] = jnp.where(mine, piece, chans[ch])
        for ch in range(11):
            chan_s[ch] = chans[ch]

    def place():
        for half in range(2):
            chans = [chan_s[ch, half * 8 : half * 8 + 8] for ch in range(11)]
            op_s[:, half * SZ : half * SZ + SZ] = columns(chans[:10], 0)
            goal_s[:, half * SZ : half * SZ + SZ] = chans[10]

    def layer_one(y):
        at = y * WIDE
        pre = dot(first_w[y], op_s[...])
        h_one_s[0:HID, at : at + WIDE] = jnp.tanh(pre[0:HID].astype(bf16))
        f_s[:, at : at + WIDE] = pre[HID : HID + 16].astype(bf16)

    def layer_two(y):
        at = y * WIDE
        pre = dot(mid_w[...], h_one_s[:, at : at + WIDE])
        h_two = jnp.tanh(pre.astype(bf16))
        h_two_s[:, at : at + WIDE] = h_two
        return dot(out_w[y], h_two)

    def errors(k, logit):
        live = jnp.where(
            (lane8 // 16) % 2 == 0, tab[2, k * CAP].astype(f32), tab[2, k * CAP + 1].astype(f32)
        )
        visc = eddy_scale * softplus(logit)
        delta = live * (visc - goal_s[...]) * eddy_scale * sigmoid(logit)
        row_s[...] = delta.astype(bf16).astype(f32)

    def output_side(y):
        at = y * WIDE
        d_s[:, at : at + WIDE] = jnp.broadcast_to(row_s[y : y + 1], (16, WIDE)).astype(bf16)
        for half in range(2):
            to = at + half * SZ
            row = jnp.broadcast_to(row_s[y : y + 1, half * SZ : half * SZ + SZ], (HID, SZ))
            act = h_two_s[:, to : to + SZ].astype(f32)
            d_two_s[:, to : to + SZ] = (out_wide * row * (1.0 - act * act)).astype(bf16)

    def input_side(y):
        at = y * WIDE
        back = dot(mid_t[...], d_two_s[:, at : at + WIDE])
        act = h_one_s[0:HID, at : at + WIDE].astype(f32)
        d_one_s[:, at : at + WIDE] = (back * (1.0 - act * act)).astype(bf16)

    def add_output(y):
        span = slice(y * WIDE, (y + 1) * WIDE)
        acc_mid[...] += dot_nt(h_one_s[:, span], d_two_s[:, span])
        acc_out[...] += dot_nt(d_s[:, span], h_two_s[:, span])

    def add_input(y):
        span = slice(y * WIDE, (y + 1) * WIDE)
        acc_in[...] += dot_nt(f_s[:, span], d_one_s[:, span])

    assemble(0)
    place()
    for y in range(8):
        layer_one(y)
    logit = jnp.zeros((16, WIDE), f32)
    for y in range(8):
        logit = logit + layer_two(y)
    errors(0, logit[:8])
    assemble(1)
    place()

    def tile(i, forward):
        @pl.when(i % 4 == 0)
        def _():
            acc_mid[...] = jnp.zeros(acc_mid.shape, f32)
            acc_in[...] = jnp.zeros(acc_in.shape, f32)
            acc_out[...] = jnp.zeros(acc_out.shape, f32)

        if forward:
            assemble(jnp.minimum(i + 2, 15))
        logit = jnp.zeros((16, WIDE), f32)
        for step in range(8 + max(LAGS)):
            at = [step - lag for lag in LAGS]
            if 0 <= at[0] < 8:
                output_side(at[0])
            if 0 <= at[1] < 8:
                input_side(at[1])
            if 0 <= at[2] < 8:
                add_output(at[2])
            if 0 <= at[3] < 8:
                add_input(at[3])
                if forward:
                    layer_one(at[3])
            if forward and 0 <= at[4] < 8:
                logit = logit + layer_two(at[4])
        if forward:
            errors((i + 1) // 4, logit[:8])
            place()

        @pl.when(i % 4 == 3)
        def _():
            k = i // 4
            stage[0:HID] = acc_mid[0:HID]
            stage[HID : HID + 1] = acc_mid[HID : HID + 1]
            stage[HID + 1 : HID + 2] = acc_in[FEAT : FEAT + 1]
            stage[HID + 2 : HID + 3] = acc_out[0:1]
            stage[HID + 8 : HID + 8 + FEAT] = acc_in[0:FEAT]
            for q in range(4):
                grads[q, k] = stage[q * QROWS : (q + 1) * QROWS]

    def one_pass(i, carry):
        tile(i, True)
        return carry

    lax.fori_loop(0, 15, one_pass, 0)
    tile(jnp.int32(15), False)


def patch_grads(gy, count, corner, dest, v, halos, target, weights, mid_t, out_col):
    return pl.pallas_call(
        patch_kernel,
        out_shape=jax.ShapeDtypeStruct((4, TRAINERS, QROWS, SZ), f32),
        in_specs=smem(4) + whole(13),
        out_specs=pl.BlockSpec(memory_space=pltpu.VMEM),
        scratch_shapes=[
            pltpu.SMEM((4, 8), jnp.int32),
            pltpu.VMEM((3, SX + 2, 48, SZ), f32),
            pltpu.VMEM((9, SX, SY, SZ), f32),
            pltpu.VMEM((SY, SZ), f32),
            pltpu.VMEM((SX, SY, SZ), f32),
            pltpu.VMEM((FEAT + 1, PATCH, SZ), f32),
            pltpu.VMEM((96, WIDE), bf16),
            pltpu.VMEM((8, WIDE), f32),
            pltpu.VMEM((HID + 16, 8 * WIDE), bf16),
            pltpu.VMEM((HID, 8 * WIDE), bf16),
            pltpu.VMEM((HID, 8 * WIDE), bf16),
            pltpu.VMEM((HID, 8 * WIDE), bf16),
            pltpu.VMEM((16, 8 * WIDE), bf16),
            pltpu.VMEM((16, 8 * WIDE), bf16),
            pltpu.VMEM((8, WIDE), f32),
            pltpu.VMEM((HID + 16, SZ), f32),
            pltpu.VMEM((16, SZ), f32),
            pltpu.VMEM((16, SZ), f32),
            pltpu.VMEM((ROWS, SZ), f32),
        ],
        compiler_params=pltpu.CompilerParams(
            vmem_limit_bytes=28 << 20
        ),
        name="patch_grads",
    )(gy, count, corner, dest, v, *halos, target, *weights, mid_t, out_col)


def gather_kernel(parts, out):
    total = parts[0]
    for i in range(1, 16):
        total = total + parts[i]
    square = jnp.sum(total * total)
    full = jnp.concatenate([total, jnp.zeros((SZ - QROWS, SZ), f32)], 0)
    out[...] = jnp.where(lanes_of((SZ, SZ)) == QROWS, square, full.T)


def scale_kernel(parts, out):
    x = parts[...].reshape(8, 2, 8, SZ)
    folded = x[:, 0] + x[:, 1]
    folded = folded.reshape(64, SZ)
    sub = sublanes_of((64, SZ))
    swapped = jnp.where(
        sub % 8 < 4, pltpu.roll(folded, 60, 0), pltpu.roll(folded, 4, 0)
    )
    norms = (folded + swapped)[:, QROWS : QROWS + 1]
    factor = jnp.broadcast_to(grad_gain / jnp.sqrt(norms + norm_epsilon), (64, SZ))
    scaled = x * factor.reshape(8, 1, 8, SZ)
    total = scaled[0]
    for i in range(1, 8):
        total = total + scaled[i]
    lane = lanes_of((1, SZ))
    quarters = []
    for q in range(4):
        rows = total[q // 2][(q % 2) * 4 : (q % 2) * 4 + 4]
        quarters.append(jnp.where(lane < QROWS, jnp.sum(rows, axis=0, keepdims=True), 0.0))
    left = quarters[0] + pltpu.roll(quarters[1], 40, 1) + pltpu.roll(quarters[2], 80, 1)
    tail = pltpu.roll(quarters[3], 120, 1)
    left = left + jnp.where(lane >= 120, tail, 0.0)
    right = jnp.where(lane < 32, tail, 0.0)
    row = jnp.concatenate([left, right], 1)
    out[...] = jnp.broadcast_to(row.reshape(1, 1, 2 * SZ), (SZ, 1, 2 * SZ))


def final_kernel(parts, mid, rest_in, bias_in, bias_mid, rest_out):
    mid[...] = parts[:, 0, 0:SZ]
    tail = parts[:, 0, SZ : 2 * SZ].T
    bias_mid[...] = tail[0:1]
    bias_in[...] = tail[1:2]
    rest_out[...] = tail[2:3]
    rest_in[...] = tail[8 : 8 + FEAT]


def call(kernel, outs, *args):
    return pl.pallas_call(
        kernel, out_shape=outs, in_specs=whole(len(args)),
        out_specs=jax.tree.map(lambda _: pl.BlockSpec(memory_space=pltpu.VMEM), outs),
        compiler_params=SMALL, name=kernel.__name__,
    )(*args)


def struct(*shape):
    return jax.ShapeDtypeStruct(shape, f32)


def bias_rows(bias):
    high = bias.astype(bf16).astype(f32)
    middle = (bias - high).astype(bf16).astype(f32)
    low = bias - high - middle
    sub = sublanes_of((16, HID))
    rows = jnp.where(sub == 0, high, jnp.where(sub == 1, middle, jnp.where(sub == 2, low, 0.0)))
    return rows.astype(bf16)


def one_hot(shape, test):
    return jnp.where(test(sublanes_of(shape), lanes_of(shape)), 1.0, 0.0).astype(bf16)


def prepare_kernel(w_in, b_in, w_mid, b_mid, w_out, first_w, mid_w, mid_t, out_w, out_col):
    eye = one_hot((HID, HID), lambda i, j: i == j)
    bias = dot_nt(eye, bias_rows(b_in[...])).astype(bf16)
    bias_part = dot(bias, one_hot((16, 96), lambda i, j: j == 80 + i))
    first = dot_nt(eye, w_in[...]).astype(bf16)
    row = jnp.broadcast_to(w_out[...], (16, HID))
    sub = sublanes_of((16, HID))
    for y in range(8):
        spread = one_hot((FEAT, 96), lambda i, j: j == i * 8 + y)
        first_w[y, 0:HID] = (dot(first, spread) + bias_part).astype(bf16)
        first_w[y, HID : HID + 16] = one_hot(
            (16, 96),
            lambda i, j: ((i < FEAT) & (j == i * 8 + y)) | ((i == FEAT) & (j == FEAT * 8)),
        )
        out_w[y] = jnp.where(sub == y, row.astype(f32), 0.0).astype(bf16)
    mid_w[:, 0:HID] = w_mid[...]
    mid_w[:, HID : HID + 16] = dot_nt(eye, bias_rows(b_mid[...])).astype(bf16)
    mid_t[...] = dot_nt(eye, w_mid[...]).astype(bf16)
    out_col[...] = dot_nt(eye, jnp.broadcast_to(w_out[...], (HID, HID)))


def prepare(weight_in, bias_in, weight_mid, bias_mid, weight_out):
    outs = [
        jax.ShapeDtypeStruct((8, HID + 16, 96), bf16),
        jax.ShapeDtypeStruct((HID, HID + 16), bf16),
        jax.ShapeDtypeStruct((HID, HID), bf16),
        jax.ShapeDtypeStruct((8, 16, HID), bf16),
        struct(HID, SZ),
    ]
    return call(
        prepare_kernel, outs, weight_in.T, bias_in.reshape(1, HID), weight_mid,
        bias_mid.reshape(1, HID), weight_out.reshape(1, HID),
    )


def on_device(
    velocity, target_visc, weight_in, bias_in, weight_mid, bias_mid, weight_out,
    patch_count, patch_corner, patch_dest,
):
    gy = lax.axis_index("gy").astype(jnp.int32).reshape(1)
    first_w, mid_w, mid_t, out_w, out_col = prepare(
        weight_in, bias_in, weight_mid, bias_mid, weight_out
    )
    net = (first_w, mid_w, out_col)
    halos = exchange(pack_faces(velocity))
    grads = patch_grads(
        gy, patch_count.reshape(1), patch_corner.reshape(SLOTS, 3).T, patch_dest.reshape(SLOTS),
        velocity, halos, target_visc, (first_w, mid_w, out_w), mid_t, out_col,
    )
    every = ("gx", "gy", "gz")
    summed = lax.all_to_all(
        grads.reshape(16, QROWS, SZ), ("gy", "gz"), split_axis=0, concat_axis=0, tiled=True
    )
    velocity_late, grads = lax.optimization_barrier((velocity, grads))
    first, *faces = section(gy, velocity_late, halos, net)
    summed, first = lax.optimization_barrier((summed, first))
    pieces = call(gather_kernel, struct(SZ, SZ), summed)
    pieces = lax.all_to_all(pieces, every, split_axis=0, concat_axis=0, tiled=True)
    halos = exchange(faces)
    pieces, halos = lax.optimization_barrier((pieces, halos))
    column = call(scale_kernel, struct(SZ, 1, 2 * SZ), pieces)
    table = lax.all_to_all(column, every, split_axis=0, concat_axis=0, tiled=True)
    first, column = lax.optimization_barrier((first, column))
    (new_velocity,) = section(gy, first, halos, net, velocity)
    table, new_velocity = lax.optimization_barrier((table, new_velocity))
    grad_mid, grad_in, grad_b_in, grad_b_mid, grad_out = call(
        final_kernel,
        [struct(HID, HID), struct(FEAT, HID), struct(1, HID), struct(1, HID), struct(1, HID)],
        table,
    )
    return (
        new_velocity, grad_in.T, grad_b_in.reshape(HID), grad_mid, grad_b_mid.reshape(HID),
        grad_out.reshape(HID),
    )


def solution(mesh):
    in_specs = (
        P(None, "gx", "gy", "gz"),
        P("gx", "gy", "gz"),
        P(), P(), P(), P(), P(),
        P("gx", "gy", "gz"),
        P("gx", "gy", "gz", None, None),
        P("gx", "gy", "gz", None),
    )
    out_specs = (P(None, "gx", "gy", "gz"), P(), P(), P(), P(), P())
    return jax.shard_map(
        on_device, mesh=mesh, in_specs=in_specs, out_specs=out_specs, check_vma=False
    )
```

```python
import jax
import jax.numpy as jnp
from jax import lax
from jax.experimental import pallas as pl
from jax.experimental.pallas import tpu as pltpu
from jax.sharding import PartitionSpec as P

SX, SY, SZ = 16, 32, 128
HID = 128
FEAT = 10
PATCH = 16
CAP = 2
TRAINERS = 4
SLOTS = CAP * TRAINERS
ROWS = 160
QROWS = ROWS // 4
WIDE = 2 * SZ
LAGS = (0, 1, 2, 3, 5)

time_step = 0.2
base_viscosity = 0.02
eddy_scale = 0.1
grad_gain = 20.0
norm_epsilon = 1e-06

SMALL = pltpu.CompilerParams(vmem_limit_bytes=8 << 20)
ROOMY = pltpu.CompilerParams(vmem_limit_bytes=24 << 20)

f32 = jnp.float32
bf16 = jnp.bfloat16


def lanes_of(shape):
    return lax.broadcasted_iota(jnp.int32, shape, len(shape) - 1)


def sublanes_of(shape):
    return lax.broadcasted_iota(jnp.int32, shape, len(shape) - 2)


def softplus(x):
    return jnp.maximum(x, 0.0) + jnp.log1p(jnp.exp(-jnp.abs(x)))


def sigmoid(x):
    e = jnp.exp(-jnp.abs(x))
    return jnp.where(x >= 0, 1.0, e) / (1.0 + e)


def dot(a, b):
    return lax.dot_general(a, b, (((1,), (0,)), ((), ())), preferred_element_type=f32)


def dot_nt(a, b):
    return lax.dot_general(a, b, (((1,), (1,)), ((), ())), preferred_element_type=f32)


def wall_plane(gy):
    rows = (gy * SY + sublanes_of((SY, SZ))).astype(f32)
    return 1.0 - jnp.abs(2.0 * (rows + 0.5) / (SY * 4) - 1.0)


def put_faces(x, planes, xlo, xhi, ylo, yhi, zlo, zhi):
    lane = lanes_of((SY, SZ))
    low, high = zlo[...], zhi[...]
    for c in range(3):
        plane = planes[c]
        ylo[c, pl.ds(x, 1), :] = plane[0:1]
        yhi[c, pl.ds(x, 1), :] = plane[SY - 1 : SY]
        here = lane == c * SX + x
        low = jnp.where(here, jnp.broadcast_to(plane[:, 0:1], (SY, SZ)), low)
        high = jnp.where(here, jnp.broadcast_to(plane[:, SZ - 1 : SZ], (SY, SZ)), high)
    zlo[...] = low
    zhi[...] = high


def faces_kernel(v, xlo, xhi, ylo, yhi, zlo, zhi):
    zlo[...] = jnp.zeros((SY, SZ), f32)
    zhi[...] = jnp.zeros((SY, SZ), f32)
    xlo[...] = v[:, 0]
    xhi[...] = v[:, SX - 1]

    def step(i, carry):
        for x in [i * 4 + j for j in range(4)]:
            put_faces(x, [v[c, x] for c in range(3)], xlo, xhi, ylo, yhi, zlo, zhi)
        return carry

    lax.fori_loop(0, SX // 4, step, 0)


FACE_SHAPES = ((3, SY, SZ),) * 2 + ((3, SX, SZ),) * 2 + ((SY, SZ),) * 2


def face_structs():
    return [jax.ShapeDtypeStruct(s, f32) for s in FACE_SHAPES]


def whole(n):
    return [pl.BlockSpec(memory_space=pltpu.VMEM) for _ in range(n)]


def smem(n):
    return [pl.BlockSpec(memory_space=pltpu.SMEM) for _ in range(n)]


def pack_faces(v):
    return pl.pallas_call(
        faces_kernel, out_shape=face_structs(), in_specs=whole(1), out_specs=whole(6), name="faces",
        compiler_params=SMALL,
    )(v)


def exchange(faces):
    xlo, xhi, ylo, yhi, zlo, zhi = faces

    def shift(low, high, axis, closed):
        count = lax.axis_size(axis)
        ends = count if closed else count - 1
        from_low = lax.ppermute(high, axis, [(i, (i + 1) % count) for i in range(ends)])
        from_high = lax.ppermute(low, axis, [((i + 1) % count, i) for i in range(ends)])
        return from_low, from_high

    return (
        shift(xlo, xhi, "gx", True) + shift(ylo, yhi, "gy", False) + shift(zlo, zhi, "gz", True)
    )


def fill_padded(v, halos, pad):
    hx0, hx1, hy0, hy1 = halos[:4]
    for c in range(3):
        pad[c, 0, 8 : 8 + SY] = hx0[c]
        pad[c, SX + 1, 8 : 8 + SY] = hx1[c]

    def step(i, carry):
        for x in [i * 4 + j for j in range(4)]:
            for c in range(3):
                pad[c, x + 1, 8 : 8 + SY] = v[c, x]
                pad[c, x + 1, 7:8] = hy0[c, pl.ds(x, 1), :]
                pad[c, x + 1, 8 + SY : 9 + SY] = hy1[c, pl.ds(x, 1), :]
        return carry

    lax.fori_loop(0, SX // 4, step, 0)


def stencil(x, pad, hz0, hz1):
    lane = lanes_of((SY, SZ))
    low, high = hz0[...], hz1[...]
    centers, dxs, dys, dzs, laps = [], [], [], [], []
    for c in range(3):
        at = c * SX + x
        ctr = pad[c, x + 1, 8 : 8 + SY]
        xm, xp = pad[c, x, 8 : 8 + SY], pad[c, x + 2, 8 : 8 + SY]
        ym, yp = pad[c, x + 1, 7 : 7 + SY], pad[c, x + 1, 9 : 9 + SY]
        zm = jnp.where(lane == 0, pltpu.roll(low, (SZ - at) % SZ, 1), pltpu.roll(ctr, 1, 1))
        zp = jnp.where(
            lane == SZ - 1, pltpu.roll(high, SZ - 1 - at, 1), pltpu.roll(ctr, SZ - 1, 1)
        )
        centers.append(ctr)
        dxs.append((xp - xm) * 0.5)
        dys.append((yp - ym) * 0.5)
        dzs.append((zp - zm) * 0.5)
        laps.append(xp + xm + yp + ym + zp + zm - 6.0 * ctr)
    return centers, dxs, dys, dzs, laps


def columns(channels, group):
    parts = [ch[group * 8 : group * 8 + 8] for ch in channels]
    parts.append(jnp.ones((16, SZ), f32))
    return jnp.concatenate(parts, 0).astype(bf16)


def section_kernel(second, *refs):
    gy = refs[0]
    v, *halos = refs[1:8]
    at = 8
    if second:
        velocity = refs[at]
        at += 1
    first_w, mid_w, out_col = refs[at : at + 3]
    at += 3
    new = refs[at]
    at += 1
    if not second:
        faces = refs[at : at + 6]
        at += 6
    pad, op_s, h_one_s, logit_s, adv_s, lap_s = refs[at : at + 6]
    fill_padded(v, halos, pad)
    wall = wall_plane(gy[0])
    h_one_s[HID : HID + 16] = jnp.ones((16, 16 * WIDE), bf16)
    if not second:
        faces[4][...] = jnp.zeros((SY, SZ), f32)
        faces[5][...] = jnp.zeros((SY, SZ), f32)

    def begin(x):
        centers, dxs, dys, dzs, laps = stencil(x, pad, halos[4], halos[5])
        chans = dxs + dys + dzs + [wall]
        for group in range(4):
            op_s[:, group * SZ : group * SZ + SZ] = columns(chans, group)
        slot = x % 4
        for c in range(3):
            adv_s[slot, c] = centers[0] * dxs[c] + centers[1] * dys[c] + centers[2] * dzs[c]
            lap_s[slot, c] = laps[c]

    def finish(x, slot):
        visc = base_viscosity + eddy_scale * softplus(logit_s[...])
        planes = []
        for c in range(3):
            rate = visc * lap_s[slot, c] - adv_s[slot, c]
            moved = pad[c, x + 1, 8 : 8 + SY] + time_step * rate
            if second:
                moved = 0.5 * velocity[c, x] + 0.5 * moved
            new[c, x] = moved
            planes.append(moved)
        if not second:
            put_faces(x, planes, *faces)

    def layer_one(i):
        operand = op_s[:, i // 8 * WIDE : i // 8 * WIDE + WIDE]
        pre = dot(first_w[i % 8, 0:HID], operand)
        h_one_s[0:HID, i * WIDE : i * WIDE + WIDE] = jnp.tanh(pre.astype(bf16))

    def layer_two(i):
        pre = dot(mid_w[...], h_one_s[:, i * WIDE : i * WIDE + WIDE])
        h_two = jnp.tanh(pre.astype(bf16)).astype(f32)
        for half in range(2):
            to = ((i // 8) * 2 + half) * 8 + i % 8
            terms = h_two[:, half * SZ : half * SZ + SZ] * out_col[...]
            logit_s[to : to + 1] = jnp.sum(terms, axis=0, keepdims=True)

    begin(0)
    for i in range(16):
        layer_one(i)
    begin(1)

    def step(x, carry):
        finish(jnp.maximum(x - 1, 0), (x + 3) % 4)
        for i in range(18):
            if i < 16:
                layer_two(i)
            if i >= 2:
                layer_one(i - 2)
        begin(jnp.minimum(x + 2, SX - 1))
        return carry

    lax.fori_loop(0, SX - 1, step, 0)
    finish(SX - 2, (SX - 2) % 4)
    for i in range(16):
        layer_two(i)
    finish(SX - 1, (SX - 1) % 4)
    if not second:
        faces[0][...] = new[:, 0]
        faces[1][...] = new[:, SX - 1]


def section(gy, v, halos, weights, velocity=None):
    second = velocity is not None
    outs = [jax.ShapeDtypeStruct((3, SX, SY, SZ), f32)]
    if not second:
        outs += face_structs()
    args = [gy, v, *halos] + ([velocity] if second else []) + list(weights)
    return pl.pallas_call(
        lambda *refs: section_kernel(second, *refs),
        out_shape=outs,
        in_specs=smem(1) + whole(len(args) - 1),
        out_specs=whole(len(outs)),
        scratch_shapes=[
            pltpu.VMEM((3, SX + 2, 48, SZ), f32),
            pltpu.VMEM((96, 4 * SZ), bf16),
            pltpu.VMEM((HID + 16, 16 * WIDE), bf16),
            pltpu.VMEM((SY, SZ), f32),
            pltpu.VMEM((4, 3, SY, SZ), f32),
            pltpu.VMEM((4, 3, SY, SZ), f32),
        ],
        compiler_params=ROOMY,
        name="section_two" if second else "section_one",
    )(*args)


def patch_kernel(
    gy, count, corner, dest, v, hx0, hx1, hy0, hy1, hz0, hz1, target,
    first_w, mid_w, out_w, mid_t, out_col, grads,
    tab, pad, feats, wall_s, tgt_s, chan_s, op_s, goal_s, h_one_s, h_two_s, d_one_s, d_two_s, f_s, d_s, row_s,
    acc_mid, acc_in, acc_out, stage,
):
    for t in range(TRAINERS):
        tab[3, t] = 0
    for s in range(SLOTS):
        d = dest[s]
        rank = tab[3, d]
        tab[3, d] = rank + 1
        spot = d * CAP + rank
        tab[0, spot] = corner[1, s]
        tab[1, spot] = corner[2, s]
        tab[2, spot] = jnp.where(s < count[0], 1, 0)
    wall_s[...] = wall_plane(gy[0])
    fill_padded(v, (hx0, hx1, hy0, hy1), pad)

    def plane(i, carry):
        for x in [i * 2, i * 2 + 1]:
            _, dxs, dys, dzs, _ = stencil(x, pad, hz0, hz1)
            for f, diff in enumerate(dxs + dys + dzs):
                feats[f, x] = diff
            tgt_s[x] = target[x].astype(f32)
        return carry

    lax.fori_loop(0, SX // 2, plane, 0)
    h_one_s[HID : HID + 16] = jnp.ones((16, 8 * WIDE), bf16)
    stage[...] = jnp.zeros((ROWS, SZ), f32)
    lane = lanes_of((PATCH, SZ))
    lane8 = lanes_of((8, WIDE))
    out_wide = out_col[...]

    def assemble(i):
        k = i // 4
        xo = i % 4
        chans = [jnp.zeros((PATCH, SZ), f32) for _ in range(11)]
        for q in range(8):
            xi, r = q // 2, q % 2
            spot = k * CAP + r
            cy, cz = tab[0, spot], tab[1, spot]
            x = xo * 4 + xi
            mine = lane // 16 == q
            turn = lax.rem(q * 16 - cz + SZ, SZ)
            for ch in range(11):
                if ch == 9:
                    piece = wall_s[pl.ds(cy, PATCH), :]
                elif ch == 10:
                    piece = tgt_s[x, pl.ds(cy, PATCH), :]
                else:
                    piece = feats[ch, x, pl.ds(cy, PATCH), :]
                if ch != 9:
                    piece = pltpu.roll(piece, turn, 1)
                chans[ch] = jnp.where(mine, piece, chans[ch])
        for ch in range(11):
            chan_s[ch] = chans[ch]

    def place():
        for half in range(2):
            chans = [chan_s[ch, half * 8 : half * 8 + 8] for ch in range(11)]
            op_s[:, half * SZ : half * SZ + SZ] = columns(chans[:10], 0)
            goal_s[:, half * SZ : half * SZ + SZ] = chans[10]

    def layer_one(y):
        at = y * WIDE
        pre = dot(first_w[y], op_s[...])
        h_one_s[0:HID, at : at + WIDE] = jnp.tanh(pre[0:HID].astype(bf16))
        f_s[:, at : at + WIDE] = pre[HID : HID + 16].astype(bf16)

    def layer_two(y):
        at = y * WIDE
        pre = dot(mid_w[...], h_one_s[:, at : at + WIDE])
        h_two = jnp.tanh(pre.astype(bf16))
        h_two_s[:, at : at + WIDE] = h_two
        return dot(out_w[y], h_two)

    def errors(k, logit):
        live = jnp.where(
            (lane8 // 16) % 2 == 0, tab[2, k * CAP].astype(f32), tab[2, k * CAP + 1].astype(f32)
        )
        visc = eddy_scale * softplus(logit)
        delta = live * (visc - goal_s[...]) * eddy_scale * sigmoid(logit)
        row_s[...] = delta.astype(bf16).astype(f32)

    def output_side(y):
        at = y * WIDE
        d_s[:, at : at + WIDE] = jnp.broadcast_to(row_s[y : y + 1], (16, WIDE)).astype(bf16)
        for half in range(2):
            to = at + half * SZ
            row = jnp.broadcast_to(row_s[y : y + 1, half * SZ : half * SZ + SZ], (HID, SZ))
            act = h_two_s[:, to : to + SZ].astype(f32)
            d_two_s[:, to : to + SZ] = (out_wide * row * (1.0 - act * act)).astype(bf16)

    def input_side(y):
        at = y * WIDE
        back = dot(mid_t[...], d_two_s[:, at : at + WIDE])
        act = h_one_s[0:HID, at : at + WIDE].astype(f32)
        d_one_s[:, at : at + WIDE] = (back * (1.0 - act * act)).astype(bf16)

    def add_output(y):
        span = slice(y * WIDE, (y + 1) * WIDE)
        acc_mid[...] += dot_nt(h_one_s[:, span], d_two_s[:, span])
        acc_out[...] += dot_nt(d_s[:, span], h_two_s[:, span])

    def add_input(y):
        span = slice(y * WIDE, (y + 1) * WIDE)
        acc_in[...] += dot_nt(f_s[:, span], d_one_s[:, span])

    assemble(0)
    place()
    for y in range(8):
        layer_one(y)
    logit = jnp.zeros((16, WIDE), f32)
    for y in range(8):
        logit = logit + layer_two(y)
    errors(0, logit[:8])
    assemble(1)
    place()

    def tile(i, forward):
        @pl.when(i % 4 == 0)
        def _():
            acc_mid[...] = jnp.zeros(acc_mid.shape, f32)
            acc_in[...] = jnp.zeros(acc_in.shape, f32)
            acc_out[...] = jnp.zeros(acc_out.shape, f32)

        if forward:
            assemble(jnp.minimum(i + 2, 15))
        logit = jnp.zeros((16, WIDE), f32)
        for step in range(8 + max(LAGS)):
            at = [step - lag for lag in LAGS]
            if 0 <= at[0] < 8:
                output_side(at[0])
            if 0 <= at[1] < 8:
                input_side(at[1])
            if 0 <= at[2] < 8:
                add_output(at[2])
            if 0 <= at[3] < 8:
                add_input(at[3])
                if forward:
                    layer_one(at[3])
            if forward and 0 <= at[4] < 8:
                logit = logit + layer_two(at[4])
        if forward:
            errors((i + 1) // 4, logit[:8])
            place()

        @pl.when(i % 4 == 3)
        def _():
            k = i // 4
            stage[0:HID] = acc_mid[0:HID]
            stage[HID : HID + 1] = acc_mid[HID : HID + 1]
            stage[HID + 1 : HID + 2] = acc_in[FEAT : FEAT + 1]
            stage[HID + 2 : HID + 3] = acc_out[0:1]
            stage[HID + 8 : HID + 8 + FEAT] = acc_in[0:FEAT]
            for q in range(4):
                grads[q, k] = stage[q * QROWS : (q + 1) * QROWS]

    def one_pass(i, carry):
        tile(i, True)
        return carry

    lax.fori_loop(0, 15, one_pass, 0)
    tile(jnp.int32(15), False)


def patch_grads(gy, count, corner, dest, v, halos, target, weights, mid_t, out_col):
    return pl.pallas_call(
        patch_kernel,
        out_shape=jax.ShapeDtypeStruct((4, TRAINERS, QROWS, SZ), f32),
        in_specs=smem(4) + whole(13),
        out_specs=pl.BlockSpec(memory_space=pltpu.VMEM),
        scratch_shapes=[
            pltpu.SMEM((4, 8), jnp.int32),
            pltpu.VMEM((3, SX + 2, 48, SZ), f32),
            pltpu.VMEM((9, SX, SY, SZ), f32),
            pltpu.VMEM((SY, SZ), f32),
            pltpu.VMEM((SX, SY, SZ), f32),
            pltpu.VMEM((FEAT + 1, PATCH, SZ), f32),
            pltpu.VMEM((96, WIDE), bf16),
            pltpu.VMEM((8, WIDE), f32),
            pltpu.VMEM((HID + 16, 8 * WIDE), bf16),
            pltpu.VMEM((HID, 8 * WIDE), bf16),
            pltpu.VMEM((HID, 8 * WIDE), bf16),
            pltpu.VMEM((HID, 8 * WIDE), bf16),
            pltpu.VMEM((16, 8 * WIDE), bf16),
            pltpu.VMEM((16, 8 * WIDE), bf16),
            pltpu.VMEM((8, WIDE), f32),
            pltpu.VMEM((HID + 16, SZ), f32),
            pltpu.VMEM((16, SZ), f32),
            pltpu.VMEM((16, SZ), f32),
            pltpu.VMEM((ROWS, SZ), f32),
        ],
        compiler_params=pltpu.CompilerParams(
            vmem_limit_bytes=28 << 20
        ),
        name="patch_grads",
    )(gy, count, corner, dest, v, *halos, target, *weights, mid_t, out_col)


def gather_kernel(parts, out):
    total = parts[0]
    for i in range(1, 16):
        total = total + parts[i]
    square = jnp.sum(total * total)
    full = jnp.concatenate([total, jnp.zeros((SZ - QROWS, SZ), f32)], 0)
    out[...] = jnp.where(lanes_of((SZ, SZ)) == QROWS, square, full.T)


def scale_kernel(parts, out):
    x = parts[...].reshape(8, 2, 8, SZ)
    folded = x[:, 0] + x[:, 1]
    folded = folded.reshape(64, SZ)
    sub = sublanes_of((64, SZ))
    swapped = jnp.where(
        sub % 8 < 4, pltpu.roll(folded, 60, 0), pltpu.roll(folded, 4, 0)
    )
    norms = (folded + swapped)[:, QROWS : QROWS + 1]
    factor = jnp.broadcast_to(grad_gain / jnp.sqrt(norms + norm_epsilon), (64, SZ))
    scaled = x * factor.reshape(8, 1, 8, SZ)
    total = scaled[0]
    for i in range(1, 8):
        total = total + scaled[i]
    lane = lanes_of((1, SZ))
    quarters = []
    for q in range(4):
        rows = total[q // 2][(q % 2) * 4 : (q % 2) * 4 + 4]
        quarters.append(jnp.where(lane < QROWS, jnp.sum(rows, axis=0, keepdims=True), 0.0))
    left = quarters[0] + pltpu.roll(quarters[1], 40, 1) + pltpu.roll(quarters[2], 80, 1)
    tail = pltpu.roll(quarters[3], 120, 1)
    left = left + jnp.where(lane >= 120, tail, 0.0)
    right = jnp.where(lane < 32, tail, 0.0)
    row = jnp.concatenate([left, right], 1)
    out[...] = jnp.broadcast_to(row.reshape(1, 1, 2 * SZ), (SZ, 1, 2 * SZ))


def final_kernel(parts, mid, rest_in, bias_in, bias_mid, rest_out):
    mid[...] = parts[:, 0, 0:SZ]
    tail = parts[:, 0, SZ : 2 * SZ].T
    bias_mid[...] = tail[0:1]
    bias_in[...] = tail[1:2]
    rest_out[...] = tail[2:3]
    rest_in[...] = tail[8 : 8 + FEAT]


def call(kernel, outs, *args):
    return pl.pallas_call(
        kernel, out_shape=outs, in_specs=whole(len(args)),
        out_specs=jax.tree.map(lambda _: pl.BlockSpec(memory_space=pltpu.VMEM), outs),
        compiler_params=SMALL, name=kernel.__name__,
    )(*args)


def struct(*shape):
    return jax.ShapeDtypeStruct(shape, f32)


def bias_rows(bias):
    high = bias.astype(bf16).astype(f32)
    middle = (bias - high).astype(bf16).astype(f32)
    low = bias - high - middle
    sub = sublanes_of((16, HID))
    rows = jnp.where(sub == 0, high, jnp.where(sub == 1, middle, jnp.where(sub == 2, low, 0.0)))
    return rows.astype(bf16)


def one_hot(shape, test):
    return jnp.where(test(sublanes_of(shape), lanes_of(shape)), 1.0, 0.0).astype(bf16)


def prepare_kernel(w_in, b_in, w_mid, b_mid, w_out, first_w, mid_w, mid_t, out_w, out_col):
    eye = one_hot((HID, HID), lambda i, j: i == j)
    bias = dot_nt(eye, bias_rows(b_in[...])).astype(bf16)
    bias_part = dot(bias, one_hot((16, 96), lambda i, j: j == 80 + i))
    first = dot_nt(eye, w_in[...]).astype(bf16)
    row = jnp.broadcast_to(w_out[...], (16, HID))
    sub = sublanes_of((16, HID))
    for y in range(8):
        spread = one_hot((FEAT, 96), lambda i, j: j == i * 8 + y)
        first_w[y, 0:HID] = (dot(first, spread) + bias_part).astype(bf16)
        first_w[y, HID : HID + 16] = one_hot(
            (16, 96),
            lambda i, j: ((i < FEAT) & (j == i * 8 + y)) | ((i == FEAT) & (j == FEAT * 8)),
        )
        out_w[y] = jnp.where(sub == y, row.astype(f32), 0.0).astype(bf16)
    mid_w[:, 0:HID] = w_mid[...]
    mid_w[:, HID : HID + 16] = dot_nt(eye, bias_rows(b_mid[...])).astype(bf16)
    mid_t[...] = dot_nt(eye, w_mid[...]).astype(bf16)
    out_col[...] = dot_nt(eye, jnp.broadcast_to(w_out[...], (HID, HID)))


def prepare(weight_in, bias_in, weight_mid, bias_mid, weight_out):
    outs = [
        jax.ShapeDtypeStruct((8, HID + 16, 96), bf16),
        jax.ShapeDtypeStruct((HID, HID + 16), bf16),
        jax.ShapeDtypeStruct((HID, HID), bf16),
        jax.ShapeDtypeStruct((8, 16, HID), bf16),
        struct(HID, SZ),
    ]
    return call(
        prepare_kernel, outs, weight_in.T, bias_in.reshape(1, HID), weight_mid,
        bias_mid.reshape(1, HID), weight_out.reshape(1, HID),
    )


def on_device(
    velocity, target_visc, weight_in, bias_in, weight_mid, bias_mid, weight_out,
    patch_count, patch_corner, patch_dest,
):
    gy = lax.axis_index("gy").astype(jnp.int32).reshape(1)
    first_w, mid_w, mid_t, out_w, out_col = prepare(
        weight_in, bias_in, weight_mid, bias_mid, weight_out
    )
    net = (first_w, mid_w, out_col)
    halos = exchange(pack_faces(velocity))
    grads = patch_grads(
        gy, patch_count.reshape(1), patch_corner.reshape(SLOTS, 3).T, patch_dest.reshape(SLOTS),
        velocity, halos, target_visc, (first_w, mid_w, out_w), mid_t, out_col,
    )
    every = ("gx", "gy", "gz")
    summed = lax.all_to_all(
        grads.reshape(16, QROWS, SZ), ("gy", "gz"), split_axis=0, concat_axis=0, tiled=True
    )
    velocity_late, grads = lax.optimization_barrier((velocity, grads))
    first, *faces = section(gy, velocity_late, halos, net)
    summed, first = lax.optimization_barrier((summed, first))
    pieces = call(gather_kernel, struct(SZ, SZ), summed)
    pieces = lax.all_to_all(pieces, every, split_axis=0, concat_axis=0, tiled=True)
    halos = exchange(faces)
    pieces, halos = lax.optimization_barrier((pieces, halos))
    column = call(scale_kernel, struct(SZ, 1, 2 * SZ), pieces)
    table = lax.all_to_all(column, every, split_axis=0, concat_axis=0, tiled=True)
    first, column = lax.optimization_barrier((first, column))
    (new_velocity,) = section(gy, first, halos, net, velocity)
    table, new_velocity = lax.optimization_barrier((table, new_velocity))
    grad_mid, grad_in, grad_b_in, grad_b_mid, grad_out = call(
        final_kernel,
        [struct(HID, HID), struct(FEAT, HID), struct(1, HID), struct(1, HID), struct(1, HID)],
        table,
    )
    return (
        new_velocity, grad_in.T, grad_b_in.reshape(HID), grad_mid, grad_b_mid.reshape(HID),
        grad_out.reshape(HID),
    )


def solution(mesh):
    in_specs = (
        P(None, "gx", "gy", "gz"),
        P("gx", "gy", "gz"),
        P(), P(), P(), P(), P(),
        P("gx", "gy", "gz"),
        P("gx", "gy", "gz", None, None),
        P("gx", "gy", "gz", None),
    )
    out_specs = (P(None, "gx", "gy", "gz"), P(), P(), P(), P(), P())
    return jax.shard_map(
        on_device, mesh=mesh, in_specs=in_specs, out_specs=out_specs, check_vma=False
    )
```
